256 devices in a mesh: dp: 2 (over z_lo), expert: 128 (over y, x, z_hi, core).
Axes of the slice: x: 4, y: 4, z: 8 (z_hi: 4, z_lo: 2; z = z_hi * 2 + z_lo), core: 2. Of those that a mesh axis runs over, the one named last changes fastest.
Arguments:
- tokens: bfloat16 [32768, 4096], P(('dp', 'expert')), may hold values from -6 to 6
- routes: int32 [256, 16, 4], P(('dp', 'expert')), may hold values from 0 to 127, as said below
- gate_values: float32 [256, 16, 4], P(('dp', 'expert')), may hold values from 0.1 to 1
- gate_weight: bfloat16 [128, 4096, 256], P('expert', 'dp'), may hold values from -0.09375 to 0.09375
- up_weight: bfloat16 [128, 4096, 256], P('expert', 'dp'), may hold values from -0.09375 to 0.09375
- down_weight: bfloat16 [128, 4096, 256], P('expert', 'dp'), may hold values from -0.125 to 0.125
- cotangent: bfloat16 [32768, 4096], P(('dp', 'expert')), may hold values from -6 to 6
Outputs:
- layer_out: bfloat16 [32768, 4096], P(('dp', 'expert'))
- token_grad: bfloat16 [32768, 4096], P(('dp', 'expert'))
- gate_grad: bfloat16 [128, 4096, 256], P('expert', 'dp')
- up_grad: bfloat16 [128, 4096, 256], P('expert', 'dp')
- down_grad: bfloat16 [128, 4096, 256], P('expert', 'dp')
The draws below stay inside these ranges and needn't reach their ends.
Inputs may be any that keep to these rules, and one draw needn't show every extreme that they name: `routes`: for each home block and each expert, 4 distinct positions within that block.
All inputs are finite; a program needn't handle non-finite values.
Results may differ from the reference program's by a relative error of at most 0.025.
Values may be sent and summed in bfloat16 or wider, within the bound.
A program may use at most 128 MiB of HBM per device.

```python
import math
import jax
import jax.numpy as jnp

D = 4096
FF = 2048
SPLIT = 8
TOK_DEV = 128
HID_DEV = 256
EXPERTS = 16
SLOT = 4
HOMES = 256
TOKENS = 32768
N_DP = 2
N_EXPERT = 128


def draw_routes(key, part):
    subkeys = jax.random.split(key, HOMES * EXPERTS)

    def pick_positions(subkey):
        return jax.random.permutation(subkey, TOK_DEV)[:SLOT]
    chosen = jax.vmap(pick_positions)(subkeys)
    return chosen.reshape(HOMES, EXPERTS, SLOT).astype(jnp.int32)


def block_levels(stream_key, dims, cuts, smallest, top_value):
    def one(axis_at, shards_of):
        steps = jax.random.uniform(jax.random.fold_in(jax.random.fold_in(stream_key, 6), axis_at), (shards_of,), jnp.float32, smallest / len(cuts), top_value / len(cuts))
        return jnp.repeat(jnp.exp(steps), dims[axis_at] // shards_of).reshape((-1,) + (1,) * (len(dims) - axis_at - 1))

    level = one(*cuts[0])
    for cut in cuts[1:]:
        level = level * one(*cut)
    return level


def bell_draw(key, extent, width, most, cuts=(), kind=jnp.bfloat16):
    entries = jax.random.normal(key, extent, jnp.float32) * width
    if len(cuts) > 0:
        entries = block_levels(key, extent, cuts, -0.22, 0.18) * entries
    return jnp.clip(entries, min=-most, max=most).astype(kind)


def setup_inputs(seed: int = 0) -> dict:
    streams_of = jax.random.split(jax.random.key(seed), 8)
    tokens = bell_draw(streams_of[0], (TOKENS, D), 1.0, 6.0, ((0, 256),))
    routes = draw_routes(jax.random.fold_in(streams_of[7], 71), 0)
    gate_values = jnp.clip(jnp.exp(math.log(1.0) - 2.3025851 * jax.random.uniform(streams_of[2], (HOMES, EXPERTS, SLOT), jnp.float32) ** block_levels(streams_of[2], (HOMES, EXPERTS, SLOT), ((0, 256),), -0.2, 0.2)), 0.1, 1.0)
    gate_weight = bell_draw(streams_of[3], (N_EXPERT, D, HID_DEV), D ** -0.5, 0.09375, ((0, 128), (1, 2)))
    up_weight = bell_draw(streams_of[4], (N_EXPERT, D, HID_DEV), D ** -0.5, 0.09375, ((0, 128), (1, 2)))
    down_weight = bell_draw(streams_of[5], (N_EXPERT, D, HID_DEV), FF ** -0.5, 0.125, ((0, 128), (1, 2)))
    cotangent = bell_draw(streams_of[6], (TOKENS, D), 1.0, 6.0, ((0, 256),))
    return dict(tokens=tokens, routes=routes, gate_values=gate_values, gate_weight=gate_weight, up_weight=up_weight, down_weight=down_weight, cotangent=cotangent)


def expert_pass(token_rows, cot_rows, gate_parts, up_parts, down_parts):
    rows_wide = token_rows.astype(jnp.float32)
    cot_wide = cot_rows.astype(jnp.float32)
    gate_wide = gate_parts.astype(jnp.float32)
    up_wide = up_parts.astype(jnp.float32)
    down_wide = down_parts.astype(jnp.float32)
    gate_pre = jnp.einsum('rd,sdh->rsh', rows_wide, gate_wide)
    up_pre = jnp.einsum('rd,sdh->rsh', rows_wide, up_wide)
    gate_sigma = jax.nn.sigmoid(gate_pre)
    hidden = (gate_pre * gate_sigma * up_pre).astype(jnp.bfloat16)
    part_out = jnp.einsum('rsh,sdh->srd', hidden.astype(jnp.float32), down_wide).astype(jnp.bfloat16)
    expert_out = jnp.sum(part_out.astype(jnp.float32), axis=0)
    hidden_grad = jnp.einsum('rd,sdh->rsh', cot_wide, down_wide)
    gate_rows = (hidden_grad * up_pre * gate_sigma * (1.0 + gate_pre * (1.0 - gate_sigma))).astype(jnp.bfloat16)
    up_rows = (hidden_grad * gate_pre * gate_sigma).astype(jnp.bfloat16)
    gate_rows_wide = gate_rows.astype(jnp.float32)
    up_rows_wide = up_rows.astype(jnp.float32)
    part_grad = (jnp.einsum('rsh,sdh->srd', gate_rows_wide, gate_wide) + jnp.einsum('rsh,sdh->srd', up_rows_wide, up_wide)).astype(jnp.bfloat16)
    row_grad = jnp.sum(part_grad.astype(jnp.float32), axis=0)
    gate_term = jnp.einsum('rd,rsh->sdh', rows_wide, gate_rows_wide)
    up_term = jnp.einsum('rd,rsh->sdh', rows_wide, up_rows_wide)
    down_term = jnp.einsum('rd,rsh->sdh', cot_wide, hidden.astype(jnp.float32))
    return expert_out, row_grad, gate_term, up_term, down_term


def reference(tokens, routes, gate_values, gate_weight, up_weight, down_weight, cotangent):
    token_blocks = tokens.reshape(N_DP, N_EXPERT, TOK_DEV, D)
    cot_blocks = cotangent.reshape(N_DP, N_EXPERT, TOK_DEV, D)
    route_blocks = routes.reshape(N_DP, N_EXPERT, EXPERTS, SLOT)
    scale_blocks = gate_values.reshape(N_DP, N_EXPERT, EXPERTS, SLOT)
    gate_parts = gate_weight.reshape(EXPERTS, SPLIT, D, HID_DEV)
    up_parts = up_weight.reshape(EXPERTS, SPLIT, D, HID_DEV)
    down_parts = down_weight.reshape(EXPERTS, SPLIT, D, HID_DEV)
    layer_out = jnp.zeros((N_DP, N_EXPERT, TOK_DEV, D), jnp.float32)
    token_grad = jnp.zeros((N_DP, N_EXPERT, TOK_DEV, D), jnp.float32)
    gate_grad = jnp.zeros((EXPERTS, SPLIT, D, HID_DEV), jnp.float32)
    up_grad = jnp.zeros((EXPERTS, SPLIT, D, HID_DEV), jnp.float32)
    down_grad = jnp.zeros((EXPERTS, SPLIT, D, HID_DEV), jnp.float32)
    home_index = jnp.arange(N_EXPERT).astype(jnp.int32)[:, None]
    for batch_index in range(N_DP):
        for expert_index in range(EXPERTS):
            chosen = route_blocks[batch_index, :, expert_index, :].astype(jnp.int32)
            scales = scale_blocks[batch_index, :, expert_index, :][:, :, None]
            picked = token_blocks[batch_index][home_index, chosen]
            cot_picked = (scales * cot_blocks[batch_index][home_index, chosen].astype(jnp.float32)).astype(jnp.bfloat16)
            expert_out, row_grad, gate_term, up_term, down_term = expert_pass(
                picked.reshape(-1, D), cot_picked.reshape(-1, D),
                gate_parts[expert_index], up_parts[expert_index], down_parts[expert_index])
            layer_out = layer_out.at[batch_index, home_index, chosen].add(scales * expert_out.reshape(N_EXPERT, SLOT, D))
            token_grad = token_grad.at[batch_index, home_index, chosen].add(row_grad.reshape(N_EXPERT, SLOT, D))
            gate_grad = gate_grad.at[expert_index].add(gate_term)
            up_grad = up_grad.at[expert_index].add(up_term)
            down_grad = down_grad.at[expert_index].add(down_term)
    return (layer_out.reshape(TOKENS, D).astype(jnp.bfloat16),
            token_grad.reshape(TOKENS, D).astype(jnp.bfloat16),
            gate_grad.reshape(N_EXPERT, D, HID_DEV).astype(jnp.bfloat16),
            up_grad.reshape(N_EXPERT, D, HID_DEV).astype(jnp.bfloat16),
            down_grad.reshape(N_EXPERT, D, HID_DEV).astype(jnp.bfloat16))
```

```python
import jax
import jax.numpy as jnp
from jax import lax
from jax.sharding import Mesh
from jax.sharding import PartitionSpec as P

SPLIT = 8
ROWS = ("dp", "yx", "col")


def send_out(payload):
    arrived = lax.all_to_all(payload, "yx", split_axis=0, concat_axis=0, tiled=True)
    shared = lax.all_gather(arrived, "col", axis=0, tiled=True)
    return shared.reshape(-1, payload.shape[-1])


def bring_back(partial_value, expert_count):
    total_rows, width = partial_value.shape
    summed = lax.psum_scatter(partial_value, "col", scatter_dimension=0, tiled=True)
    summed = summed.reshape(expert_count, -1, width)
    returned = lax.all_to_all(summed, "yx", split_axis=0, concat_axis=0, tiled=True)
    return returned.astype(jnp.float32)


def shards(tokens, routes, gate_values, gate_weight, up_weight, down_weight, cotangent):
    width = tokens.shape[1]
    expert_count = routes.shape[1]
    chosen = routes[0]
    scales = gate_values[0][:, :, None]
    contract_last = (((1,), (1,)), ((), ()))
    contract_first = (((0,), (0,)), ((), ()))
    full_gate, full_up, full_down = (
        lax.all_gather(gate_weight, "dp", axis=1, tiled=True),
        lax.all_gather(up_weight, "dp", axis=1, tiled=True),
        lax.all_gather(down_weight, "dp", axis=1, tiled=True),
    )
    full_gate = full_gate[0]
    full_up = full_up[0]
    full_down = full_down[0]
    token_rows = send_out(tokens[chosen])
    scaled_cot = (scales * cotangent[chosen].astype(jnp.float32)).astype(jnp.bfloat16)
    cot_rows = send_out(scaled_cot)
    gate_pre = jnp.dot(token_rows, full_gate, preferred_element_type=jnp.float32)
    up_pre = jnp.dot(token_rows, full_up, preferred_element_type=jnp.float32)
    gate_sigma = jax.nn.sigmoid(gate_pre)
    hidden = (gate_pre * gate_sigma * up_pre).astype(jnp.bfloat16)
    partial_value = lax.dot_general(
        hidden, full_down, contract_last, preferred_element_type=jnp.float32
    ).astype(jnp.bfloat16)
    combined = bring_back(partial_value, expert_count)
    layer_out = jnp.zeros((tokens.shape[0], width), jnp.float32).at[chosen].add(scales * combined)
    hidden_grad = jnp.dot(cot_rows, full_down, preferred_element_type=jnp.float32)
    gate_rows = (hidden_grad * up_pre * gate_sigma * (1.0 + gate_pre * (1.0 - gate_sigma))).astype(
        jnp.bfloat16
    )
    up_rows = (hidden_grad * gate_pre * gate_sigma).astype(jnp.bfloat16)
    partial_grad = (
        lax.dot_general(gate_rows, full_gate, contract_last, preferred_element_type=jnp.float32)
        + lax.dot_general(up_rows, full_up, contract_last, preferred_element_type=jnp.float32)
    ).astype(jnp.bfloat16)
    token_grad = (
        jnp.zeros((tokens.shape[0], width), jnp.float32)
        .at[chosen]
        .add(bring_back(partial_grad, expert_count))
    )
    grad_sums = lax.psum_scatter(
        jnp.concatenate(
            [
                lax.dot_general(
                    token_rows, gate_rows, contract_first, preferred_element_type=jnp.float32
                ),
                lax.dot_general(
                    token_rows, up_rows, contract_first, preferred_element_type=jnp.float32
                ),
                lax.dot_general(
                    cot_rows, hidden, contract_first, preferred_element_type=jnp.float32
                ),
            ],
            axis=1,
        ).astype(jnp.bfloat16),
        "dp",
        scatter_dimension=0,
        tiled=True,
    ).astype(jnp.float32)
    hidden_width = hidden.shape[1]
    gate_grad = grad_sums[:, :hidden_width].astype(jnp.bfloat16)[None]
    up_grad = grad_sums[:, hidden_width : 2 * hidden_width].astype(jnp.bfloat16)[None]
    down_grad = grad_sums[:, 2 * hidden_width :].astype(jnp.bfloat16)[None]
    return (
        layer_out.astype(jnp.bfloat16),
        token_grad.astype(jnp.bfloat16),
        gate_grad,
        up_grad,
        down_grad,
    )


def solution(mesh):
    n_dp, n_expert = mesh.devices.shape
    fine = Mesh(mesh.devices.reshape(n_dp, n_expert // SPLIT, SPLIT), ROWS)
    placed = (
        P(ROWS, None),
        P(ROWS, None, None),
        P(ROWS, None, None),
        P(("yx", "col"), "dp", None),
        P(("yx", "col"), "dp", None),
        P(("yx", "col"), "dp", None),
        P(ROWS, None),
    )
    return jax.shard_map(
        shards,
        mesh=fine,
        in_specs=placed,
        out_specs=(
            P(ROWS, None),
            P(ROWS, None),
            P(("yx", "col"), "dp", None),
            P(("yx", "col"), "dp", None),
            P(("yx", "col"), "dp", None),
        ),
        check_vma=False,
    )
```

```python
import jax
import jax.numpy as jnp
from jax import lax
from jax.sharding import Mesh
from jax.sharding import PartitionSpec as P

SPLIT = 8
ROWS = ("dp", "yx", "col")


def send_out(payload):
    arrived = lax.all_to_all(payload, "yx", split_axis=1, concat_axis=1, tiled=True)
    shared = lax.all_gather(arrived, "col", axis=1, tiled=True)
    return shared.reshape(payload.shape[0], -1, payload.shape[-1])


def bring_back(partial_value, expert_count):
    streams, total_rows, width = partial_value.shape
    summed = lax.psum_scatter(partial_value, "col", scatter_dimension=1, tiled=True)
    summed = summed.reshape(streams, expert_count, -1, width)
    returned = lax.all_to_all(summed, "yx", split_axis=1, concat_axis=1, tiled=True)
    return returned.astype(jnp.float32)


def shards(tokens, routes, gate_values, gate_weight, up_weight, down_weight, cotangent):
    width = tokens.shape[1]
    expert_count = routes.shape[1]
    chosen = routes[0]
    scales = gate_values[0][:, :, None]
    contract_last = (((1,), (1,)), ((), ()))
    contract_first = (((0,), (0,)), ((), ()))
    weights = jnp.concatenate([gate_weight, up_weight, down_weight], axis=0)
    full = lax.all_gather(weights, "dp", axis=1, tiled=True)
    full_gate, full_up, full_down = full[0], full[1], full[2]
    scaled_cot = (scales * cotangent[chosen].astype(jnp.float32)).astype(jnp.bfloat16)
    both_rows = send_out(jnp.stack([tokens[chosen], scaled_cot]))
    token_rows, cot_rows = both_rows[0], both_rows[1]
    gate_pre = jnp.dot(token_rows, full_gate, preferred_element_type=jnp.float32)
    up_pre = jnp.dot(token_rows, full_up, preferred_element_type=jnp.float32)
    gate_sigma = jax.nn.sigmoid(gate_pre)
    hidden = (gate_pre * gate_sigma * up_pre).astype(jnp.bfloat16)
    partial_value = lax.dot_general(
        hidden, full_down, contract_last, preferred_element_type=jnp.float32
    ).astype(jnp.bfloat16)
    hidden_grad = jnp.dot(cot_rows, full_down, preferred_element_type=jnp.float32)
    gate_rows = (hidden_grad * up_pre * gate_sigma * (1.0 + gate_pre * (1.0 - gate_sigma))).astype(
        jnp.bfloat16
    )
    up_rows = (hidden_grad * gate_pre * gate_sigma).astype(jnp.bfloat16)
    partial_grad = (
        lax.dot_general(gate_rows, full_gate, contract_last, preferred_element_type=jnp.float32)
        + lax.dot_general(up_rows, full_up, contract_last, preferred_element_type=jnp.float32)
    ).astype(jnp.bfloat16)
    back = bring_back(jnp.stack([partial_value, partial_grad]), expert_count)
    layer_out = jnp.zeros((tokens.shape[0], width), jnp.float32).at[chosen].add(scales * back[0])
    token_grad = jnp.zeros((tokens.shape[0], width), jnp.float32).at[chosen].add(back[1])
    grad_sums = lax.psum_scatter(
        jnp.concatenate(
            [
                lax.dot_general(
                    token_rows, gate_rows, contract_first, preferred_element_type=jnp.float32
                ),
                lax.dot_general(
                    token_rows, up_rows, contract_first, preferred_element_type=jnp.float32
                ),
                lax.dot_general(
                    cot_rows, hidden, contract_first, preferred_element_type=jnp.float32
                ),
            ],
            axis=1,
        ).astype(jnp.bfloat16),
        "dp",
        scatter_dimension=0,
        tiled=True,
    ).astype(jnp.float32)
    hidden_width = hidden.shape[1]
    gate_grad = grad_sums[:, :hidden_width].astype(jnp.bfloat16)[None]
    up_grad = grad_sums[:, hidden_width : 2 * hidden_width].astype(jnp.bfloat16)[None]
    down_grad = grad_sums[:, 2 * hidden_width :].astype(jnp.bfloat16)[None]
    return (
        layer_out.astype(jnp.bfloat16),
        token_grad.astype(jnp.bfloat16),
        gate_grad,
        up_grad,
        down_grad,
    )


def solution(mesh):
    n_dp, n_expert = mesh.devices.shape
    fine = Mesh(mesh.devices.reshape(n_dp, n_expert // SPLIT, SPLIT), ROWS)
    placed = (
        P(ROWS, None),
        P(ROWS, None, None),
        P(ROWS, None, None),
        P(("yx", "col"), "dp", None),
        P(("yx", "col"), "dp", None),
        P(("yx", "col"), "dp", None),
        P(ROWS, None),
    )
    return jax.shard_map(
        shards,
        mesh=fine,
        in_specs=placed,
        out_specs=(
            P(ROWS, None),
            P(ROWS, None),
            P(("yx", "col"), "dp", None),
            P(("yx", "col"), "dp", None),
            P(("yx", "col"), "dp", None),
        ),
        check_vma=False,
    )
```

```python
import jax
import jax.numpy as jnp
from jax import lax
from jax.experimental import pallas as pl
from jax.experimental.pallas import tpu as pltpu
from jax.sharding import Mesh
from jax.sharding import PartitionSpec as P

SPLIT = 8
ROWS = ("dp", "yx", "col")
MESH_ID = pl.DeviceIdType.MESH


def swap_kernel(src_ref, dst_ref, sems):
    other = 1 - lax.axis_index("dp")
    barrier = pltpu.get_barrier_semaphore()
    pl.semaphore_signal(barrier, 1, device_id={"dp": other}, device_id_type=MESH_ID)
    pl.semaphore_wait(barrier, 1)
    copy = pltpu.make_async_remote_copy(
        src_ref=src_ref,
        dst_ref=dst_ref,
        send_sem=sems.at[0],
        recv_sem=sems.at[1],
        device_id={"dp": other},
        device_id_type=MESH_ID,
    )
    copy.start()
    copy.wait()


def swap_with_partner(x, collective_id):
    size = x.size * x.dtype.itemsize
    return pl.pallas_call(
        swap_kernel,
        out_shape=jax.ShapeDtypeStruct(x.shape, x.dtype),
        in_specs=[pl.BlockSpec(memory_space=pl.ANY)],
        out_specs=pl.BlockSpec(memory_space=pl.ANY),
        scratch_shapes=[pltpu.SemaphoreType.DMA((2,))],
        compiler_params=pltpu.CompilerParams(collective_id=collective_id, has_side_effects=True),
        cost_estimate=pl.CostEstimate(flops=0, bytes_accessed=2 * size, transcendentals=0),
    )(x)


def send_out(payload):
    arrived = lax.all_to_all(payload, "yx", split_axis=1, concat_axis=1, tiled=True)
    shared = lax.all_gather(arrived, "col", axis=1, tiled=True)
    return shared.reshape(payload.shape[0], -1, payload.shape[-1])


def bring_back(partial_value, expert_count):
    streams, total_rows, width = partial_value.shape
    summed = lax.psum_scatter(partial_value, "col", scatter_dimension=1, tiled=True)
    summed = summed.reshape(streams, expert_count, -1, width)
    return lax.all_to_all(summed, "yx", split_axis=1, concat_axis=1, tiled=True)


def shards(tokens, routes, gate_values, gate_weight, up_weight, down_weight, cotangent):
    width = tokens.shape[1]
    half = gate_weight.shape[1]
    expert_count = routes.shape[1]
    chosen = routes[0]
    scales = gate_values[0][:, :, None]
    contract_last = (((1,), (1,)), ((), ()))
    contract_first = (((0,), (0,)), ((), ()))
    shift = lax.axis_index("dp") * half
    own = jnp.concatenate([gate_weight, up_weight, down_weight], axis=0)
    other = swap_with_partner(own, 0)
    full = jnp.concatenate([own, other], axis=1)
    full_gate, full_up, full_down = full[0], full[1], full[2]
    scaled_cot = (scales * cotangent[chosen].astype(jnp.float32)).astype(jnp.bfloat16)
    home_rows = jnp.roll(jnp.stack([tokens[chosen], scaled_cot]), -shift, axis=-1)
    both_rows = send_out(home_rows)
    token_rows, cot_rows = both_rows[0], both_rows[1]
    gate_pre = jnp.dot(token_rows, full_gate, preferred_element_type=jnp.float32)
    up_pre = jnp.dot(token_rows, full_up, preferred_element_type=jnp.float32)
    gate_sigma = jax.nn.sigmoid(gate_pre)
    hidden = (gate_pre * gate_sigma * up_pre).astype(jnp.bfloat16)
    partial_value = lax.dot_general(
        hidden, full_down, contract_last, preferred_element_type=jnp.float32
    ).astype(jnp.bfloat16)
    hidden_grad = jnp.dot(cot_rows, full_down, preferred_element_type=jnp.float32)
    gate_rows = (hidden_grad * up_pre * gate_sigma * (1.0 + gate_pre * (1.0 - gate_sigma))).astype(
        jnp.bfloat16
    )
    up_rows = (hidden_grad * gate_pre * gate_sigma).astype(jnp.bfloat16)
    partial_grad = (
        lax.dot_general(gate_rows, full_gate, contract_last, preferred_element_type=jnp.float32)
        + lax.dot_general(up_rows, full_up, contract_last, preferred_element_type=jnp.float32)
    ).astype(jnp.bfloat16)
    back = bring_back(jnp.stack([partial_value, partial_grad]), expert_count)
    back = jnp.roll(back, shift, axis=-1).astype(jnp.float32)
    layer_out = jnp.zeros((tokens.shape[0], width), jnp.float32).at[chosen].add(scales * back[0])
    token_grad = jnp.zeros((tokens.shape[0], width), jnp.float32).at[chosen].add(back[1])
    grad_terms = jnp.stack(
        [
            lax.dot_general(token_rows, gate_rows, contract_first, preferred_element_type=jnp.float32),
            lax.dot_general(token_rows, up_rows, contract_first, preferred_element_type=jnp.float32),
            lax.dot_general(cot_rows, hidden, contract_first, preferred_element_type=jnp.float32),
        ]
    )
    arrived = swap_with_partner(grad_terms[:, half:].astype(jnp.bfloat16), 1)
    grad_sums = (grad_terms[:, :half] + arrived.astype(jnp.float32)).astype(jnp.bfloat16)
    return (
        layer_out.astype(jnp.bfloat16),
        token_grad.astype(jnp.bfloat16),
        grad_sums[0][None],
        grad_sums[1][None],
        grad_sums[2][None],
    )


def solution(mesh):
    n_dp, n_expert = mesh.devices.shape
    fine = Mesh(mesh.devices.reshape(n_dp, n_expert // SPLIT, SPLIT), ROWS)
    placed = (
        P(ROWS, None),
        P(ROWS, None, None),
        P(ROWS, None, None),
        P(("yx", "col"), "dp", None),
        P(("yx", "col"), "dp", None),
        P(("yx", "col"), "dp", None),
        P(ROWS, None),
    )
    return jax.shard_map(
        shards,
        mesh=fine,
        in_specs=placed,
        out_specs=(
            P(ROWS, None),
            P(ROWS, None),
            P(("yx", "col"), "dp", None),
            P(("yx", "col"), "dp", None),
            P(("yx", "col"), "dp", None),
        ),
        check_vma=False,
    )
```

```python
import jax
import jax.numpy as jnp
from jax import lax
from jax.experimental import pallas as pl
from jax.experimental.pallas import tpu as pltpu
from jax.sharding import Mesh
from jax.sharding import PartitionSpec as P

SPLIT = 8
ROWS = ("dp", "yx", "col")
MESH_ID = pl.DeviceIdType.MESH


def swap_kernel(src_ref, dst_ref, sems):
    other = 1 - lax.axis_index("dp")
    barrier = pltpu.get_barrier_semaphore()
    pl.semaphore_signal(barrier, 1, device_id={"dp": other}, device_id_type=MESH_ID)
    pl.semaphore_wait(barrier, 1)
    copy = pltpu.make_async_remote_copy(
        src_ref=src_ref,
        dst_ref=dst_ref,
        send_sem=sems.at[0],
        recv_sem=sems.at[1],
        device_id={"dp": other},
        device_id_type=MESH_ID,
    )
    copy.start()
    copy.wait()


def swap_with_partner(x, collective_id):
    size = x.size * x.dtype.itemsize
    return pl.pallas_call(
        swap_kernel,
        out_shape=jax.ShapeDtypeStruct(x.shape, x.dtype),
        in_specs=[pl.BlockSpec(memory_space=pl.ANY)],
        out_specs=pl.BlockSpec(memory_space=pl.ANY),
        scratch_shapes=[pltpu.SemaphoreType.DMA((2,))],
        compiler_params=pltpu.CompilerParams(collective_id=collective_id, has_side_effects=True),
        cost_estimate=pl.CostEstimate(flops=0, bytes_accessed=2 * size, transcendentals=0),
    )(x)


def send_out(payload):
    arrived = lax.all_to_all(payload, "yx", split_axis=1, concat_axis=1, tiled=True)
    shared = lax.all_gather(arrived, "col", axis=1, tiled=True)
    return shared.reshape(payload.shape[0], -1, payload.shape[-1])


def bring_back(partial_value, expert_count):
    streams, total_rows, width = partial_value.shape
    summed = lax.psum_scatter(partial_value, "col", scatter_dimension=1, tiled=True)
    summed = summed.reshape(streams, expert_count, -1, width)
    return lax.all_to_all(summed, "yx", split_axis=1, concat_axis=1, tiled=True)


def shards(tokens, routes, gate_values, gate_weight, up_weight, down_weight, cotangent):
    width = tokens.shape[1]
    half = gate_weight.shape[1]
    expert_count = routes.shape[1]
    chosen = routes[0]
    scales = gate_values[0][:, :, None]
    contract_last = (((1,), (1,)), ((), ()))
    contract_first = (((0,), (0,)), ((), ()))
    shift = lax.axis_index("dp") * half
    own = jnp.concatenate([gate_weight, up_weight, down_weight], axis=0)
    other = swap_with_partner(own, 0)
    full = jnp.concatenate([own, other], axis=1)
    full_gate, full_up, full_down = full[0], full[1], full[2]
    scaled_cot = (scales * cotangent[chosen].astype(jnp.float32)).astype(jnp.bfloat16)
    token_rows = send_out(jnp.roll(tokens[chosen], -shift, axis=-1)[None])[0]
    cot_rows = send_out(jnp.roll(scaled_cot, -shift, axis=-1)[None])[0]
    gate_pre = jnp.dot(token_rows, full_gate, preferred_element_type=jnp.float32)
    up_pre = jnp.dot(token_rows, full_up, preferred_element_type=jnp.float32)
    gate_sigma = jax.nn.sigmoid(gate_pre)
    hidden = (gate_pre * gate_sigma * up_pre).astype(jnp.bfloat16)
    partial_value = lax.dot_general(
        hidden, full_down, contract_last, preferred_element_type=jnp.float32
    ).astype(jnp.bfloat16)
    hidden_grad = jnp.dot(cot_rows, full_down, preferred_element_type=jnp.float32)
    gate_rows = (hidden_grad * up_pre * gate_sigma * (1.0 + gate_pre * (1.0 - gate_sigma))).astype(
        jnp.bfloat16
    )
    up_rows = (hidden_grad * gate_pre * gate_sigma).astype(jnp.bfloat16)
    partial_grad = (
        lax.dot_general(gate_rows, full_gate, contract_last, preferred_element_type=jnp.float32)
        + lax.dot_general(up_rows, full_up, contract_last, preferred_element_type=jnp.float32)
    ).astype(jnp.bfloat16)
    back_value = bring_back(partial_value[None], expert_count)[0]
    back_value = jnp.roll(back_value, shift, axis=-1).astype(jnp.float32)
    back_grad = bring_back(partial_grad[None], expert_count)[0]
    back_grad = jnp.roll(back_grad, shift, axis=-1).astype(jnp.float32)
    layer_out = jnp.zeros((tokens.shape[0], width), jnp.float32).at[chosen].add(scales * back_value)
    token_grad = jnp.zeros((tokens.shape[0], width), jnp.float32).at[chosen].add(back_grad)
    grad_terms = jnp.stack(
        [
            lax.dot_general(token_rows, gate_rows, contract_first, preferred_element_type=jnp.float32),
            lax.dot_general(token_rows, up_rows, contract_first, preferred_element_type=jnp.float32),
            lax.dot_general(cot_rows, hidden, contract_first, preferred_element_type=jnp.float32),
        ]
    )
    arrived = swap_with_partner(grad_terms[:, half:].astype(jnp.bfloat16), 1)
    grad_sums = (grad_terms[:, :half] + arrived.astype(jnp.float32)).astype(jnp.bfloat16)
    return (
        layer_out.astype(jnp.bfloat16),
        token_grad.astype(jnp.bfloat16),
        grad_sums[0][None],
        grad_sums[1][None],
        grad_sums[2][None],
    )


def solution(mesh):
    n_dp, n_expert = mesh.devices.shape
    fine = Mesh(mesh.devices.reshape(n_dp, n_expert // SPLIT, SPLIT), ROWS)
    placed = (
        P(ROWS, None),
        P(ROWS, None, None),
        P(ROWS, None, None),
        P(("yx", "col"), "dp", None),
        P(("yx", "col"), "dp", None),
        P(("yx", "col"), "dp", None),
        P(ROWS, None),
    )
    return jax.shard_map(
        shards,
        mesh=fine,
        in_specs=placed,
        out_specs=(
            P(ROWS, None),
            P(ROWS, None),
            P(("yx", "col"), "dp", None),
            P(("yx", "col"), "dp", None),
            P(("yx", "col"), "dp", None),
        ),
        check_vma=False,
    )
```

```python
import jax
import jax.numpy as jnp
from jax import lax
from jax.experimental import pallas as pl
from jax.experimental.pallas import tpu as pltpu
from jax.sharding import Mesh
from jax.sharding import PartitionSpec as P

SPLIT = 8
ROWS = ("dp", "yx", "col")
MESH_ID = pl.DeviceIdType.MESH
CONTRACT_LAST = (((1,), (1,)), ((), ()))
CONTRACT_FIRST = (((0,), (0,)), ((), ()))


def swap_kernel(src_ref, dst_ref, sems):
    other = 1 - lax.axis_index("dp")
    barrier = pltpu.get_barrier_semaphore()
    pl.semaphore_signal(barrier, 1, device_id={"dp": other}, device_id_type=MESH_ID)
    pl.semaphore_wait(barrier, 1)
    copy = pltpu.make_async_remote_copy(
        src_ref=src_ref,
        dst_ref=dst_ref,
        send_sem=sems.at[0],
        recv_sem=sems.at[1],
        device_id={"dp": other},
        device_id_type=MESH_ID,
    )
    copy.start()
    copy.wait()


def swap_with_partner(x, collective_id):
    size = x.size * x.dtype.itemsize
    return pl.pallas_call(
        swap_kernel,
        out_shape=jax.ShapeDtypeStruct(x.shape, x.dtype),
        in_specs=[pl.BlockSpec(memory_space=pl.ANY)],
        out_specs=pl.BlockSpec(memory_space=pl.ANY),
        scratch_shapes=[pltpu.SemaphoreType.DMA((2,))],
        compiler_params=pltpu.CompilerParams(collective_id=collective_id, has_side_effects=True),
        cost_estimate=pl.CostEstimate(flops=0, bytes_accessed=2 * size, transcendentals=0),
    )(x)


def send_out(payload, shift, half, collective_id):
    arrived = lax.all_to_all(payload[None], "yx", split_axis=1, concat_axis=1, tiled=True)[0]
    rolled = jnp.roll(arrived, -shift, axis=-1)
    traded = swap_with_partner(rolled[..., half:], collective_id)
    both = jnp.stack([rolled[..., :half], traded])
    shared = lax.all_gather(both, "col", axis=0, tiled=False)
    return shared.reshape(-1, half)


def bring_back(partial_rows, shift, collective_id):
    total_rows, half = partial_rows.shape
    summed = lax.psum_scatter(
        partial_rows.reshape(SPLIT, 2, -1, half), "col", scatter_dimension=0, tiled=True
    )[0]
    traded = swap_with_partner(summed[1], collective_id)
    rows = jnp.roll(jnp.concatenate([summed[0], traded], axis=-1), shift, axis=-1)
    rows = rows.reshape(-1, 4, 2 * half)
    back = lax.all_to_all(rows[None], "yx", split_axis=1, concat_axis=1, tiled=True)[0]
    return back.astype(jnp.float32)


def own_batch(partial, collective_id):
    rows, k = partial.shape
    split = partial.reshape(SPLIT, 2, -1, k)
    traded = swap_with_partner(split[:, 1], collective_id)
    return (split[:, 0] + traded).reshape(-1, k)


def both_batches(values, collective_id):
    traded = swap_with_partner(values, collective_id)
    lead = values.shape[:-2]
    k = values.shape[-1]
    mine = values.reshape(lead + (SPLIT, 1, -1, k))
    theirs = traded.reshape(lead + (SPLIT, 1, -1, k))
    return jnp.concatenate([mine, theirs], axis=-3).reshape(lead + (-1, k))


def shards(tokens, routes, gate_values, gate_weight, up_weight, down_weight, cotangent):
    width = tokens.shape[1]
    half = gate_weight.shape[1]
    chosen = routes[0]
    scales = gate_values[0][:, :, None]
    shift = lax.axis_index("dp") * half
    wg, wu, wd = gate_weight[0], up_weight[0], down_weight[0]
    scaled_cot = (scales * cotangent[chosen].astype(jnp.float32)).astype(jnp.bfloat16)
    token_rows = send_out(tokens[chosen], shift, half, 0)
    cot_rows = send_out(scaled_cot, shift, half, 1)
    gate_pre = own_batch(jnp.dot(token_rows, wg, preferred_element_type=jnp.float32), 2)
    up_pre = own_batch(jnp.dot(token_rows, wu, preferred_element_type=jnp.float32), 3)
    gate_sigma = jax.nn.sigmoid(gate_pre)
    hidden = (gate_pre * gate_sigma * up_pre).astype(jnp.bfloat16)
    hidden_all = both_batches(hidden, 4)
    partial_value = lax.dot_general(
        hidden_all, wd, CONTRACT_LAST, preferred_element_type=jnp.float32
    ).astype(jnp.bfloat16)
    back_value = bring_back(partial_value, shift, 5)
    hidden_grad = own_batch(jnp.dot(cot_rows, wd, preferred_element_type=jnp.float32), 6)
    gate_rows = (hidden_grad * up_pre * gate_sigma * (1.0 + gate_pre * (1.0 - gate_sigma))).astype(
        jnp.bfloat16
    )
    up_rows = (hidden_grad * gate_pre * gate_sigma).astype(jnp.bfloat16)
    rows_all = both_batches(jnp.stack([gate_rows, up_rows]), 7)
    gate_all, up_all = rows_all[0], rows_all[1]
    partial_grad = (
        lax.dot_general(gate_all, wg, CONTRACT_LAST, preferred_element_type=jnp.float32)
        + lax.dot_general(up_all, wu, CONTRACT_LAST, preferred_element_type=jnp.float32)
    ).astype(jnp.bfloat16)
    back_grad = bring_back(partial_grad, shift, 8)
    layer_out = jnp.zeros((tokens.shape[0], width), jnp.float32).at[chosen].add(scales * back_value)
    token_grad = jnp.zeros((tokens.shape[0], width), jnp.float32).at[chosen].add(back_grad)
    gate_grad = lax.dot_general(token_rows, gate_all, CONTRACT_FIRST, preferred_element_type=jnp.float32)
    up_grad = lax.dot_general(token_rows, up_all, CONTRACT_FIRST, preferred_element_type=jnp.float32)
    down_grad = lax.dot_general(cot_rows, hidden_all, CONTRACT_FIRST, preferred_element_type=jnp.float32)
    return (
        layer_out.astype(jnp.bfloat16),
        token_grad.astype(jnp.bfloat16),
        gate_grad.astype(jnp.bfloat16)[None],
        up_grad.astype(jnp.bfloat16)[None],
        down_grad.astype(jnp.bfloat16)[None],
    )


def solution(mesh):
    n_dp, n_expert = mesh.devices.shape
    fine = Mesh(mesh.devices.reshape(n_dp, n_expert // SPLIT, SPLIT), ROWS)
    placed = (
        P(ROWS, None),
        P(ROWS, None, None),
        P(ROWS, None, None),
        P(("yx", "col"), "dp", None),
        P(("yx", "col"), "dp", None),
        P(("yx", "col"), "dp", None),
        P(ROWS, None),
    )
    return jax.shard_map(
        shards,
        mesh=fine,
        in_specs=placed,
        out_specs=(
            P(ROWS, None),
            P(ROWS, None),
            P(("yx", "col"), "dp", None),
            P(("yx", "col"), "dp", None),
            P(("yx", "col"), "dp", None),
        ),
        check_vma=False,
    )
```

```python
import jax
import jax.numpy as jnp
from jax import lax
from jax.experimental import pallas as pl
from jax.experimental.pallas import tpu as pltpu
from jax.sharding import Mesh
from jax.sharding import PartitionSpec as P

SPLIT = 8
ROWS = ("dp", "yx", "col")
MESH_ID = pl.DeviceIdType.MESH
CONTRACT_LAST = (((1,), (1,)), ((), ()))
CONTRACT_FIRST = (((0,), (0,)), ((), ()))


def swap_kernel(src_ref, dst_ref, sems):
    other = 1 - lax.axis_index("dp")
    barrier = pltpu.get_barrier_semaphore()
    pl.semaphore_signal(barrier, 1, device_id={"dp": other}, device_id_type=MESH_ID)
    pl.semaphore_wait(barrier, 1)
    copy = pltpu.make_async_remote_copy(
        src_ref=src_ref,
        dst_ref=dst_ref,
        send_sem=sems.at[0],
        recv_sem=sems.at[1],
        device_id={"dp": other},
        device_id_type=MESH_ID,
    )
    copy.start()
    copy.wait()


def swap_with_partner(x, collective_id):
    size = x.size * x.dtype.itemsize
    return pl.pallas_call(
        swap_kernel,
        out_shape=jax.ShapeDtypeStruct(x.shape, x.dtype),
        in_specs=[pl.BlockSpec(memory_space=pl.ANY)],
        out_specs=pl.BlockSpec(memory_space=pl.ANY),
        scratch_shapes=[pltpu.SemaphoreType.DMA((2,))],
        compiler_params=pltpu.CompilerParams(collective_id=collective_id, has_side_effects=True),
        cost_estimate=pl.CostEstimate(flops=0, bytes_accessed=2 * size, transcendentals=0),
    )(x)


def send_out(payload, shift, half, collective_id):
    arrived = lax.all_to_all(payload, "yx", split_axis=1, concat_axis=1, tiled=True)
    rolled = jnp.roll(arrived, -shift, axis=-1)
    traded = swap_with_partner(rolled[..., half:], collective_id)
    both = jnp.stack([rolled[..., :half], traded], axis=1)
    shared = lax.all_gather(both, "col", axis=1, tiled=False)
    return shared.reshape(payload.shape[0], -1, half)


def bring_back(partial_rows, shift, collective_id):
    streams, total_rows, half = partial_rows.shape
    summed = lax.psum_scatter(
        partial_rows.reshape(streams, SPLIT, 2, -1, half), "col", scatter_dimension=1, tiled=True
    )[:, 0]
    traded = swap_with_partner(summed[:, 1], collective_id)
    rows = jnp.roll(jnp.concatenate([summed[:, 0], traded], axis=-1), shift, axis=-1)
    back = lax.all_to_all(rows, "yx", split_axis=1, concat_axis=1, tiled=True)
    return back.astype(jnp.float32)


def own_batch(partial, collective_id):
    streams, rows, k = partial.shape
    split = partial.reshape(streams, SPLIT, 2, -1, k)
    traded = swap_with_partner(split[:, :, 1], collective_id)
    return (split[:, :, 0] + traded).reshape(streams, -1, k)


def both_batches(values, collective_id):
    traded = swap_with_partner(values, collective_id)
    streams, rows, k = values.shape
    mine = values.reshape(streams, SPLIT, 1, -1, k)
    theirs = traded.reshape(streams, SPLIT, 1, -1, k)
    return jnp.concatenate([mine, theirs], axis=2).reshape(streams, -1, k)


def shards(tokens, routes, gate_values, gate_weight, up_weight, down_weight, cotangent):
    width = tokens.shape[1]
    half = gate_weight.shape[1]
    chosen = routes[0]
    scales = gate_values[0][:, :, None]
    shift = lax.axis_index("dp") * half
    wg, wu, wd = gate_weight[0], up_weight[0], down_weight[0]
    scaled_cot = (scales * cotangent[chosen].astype(jnp.float32)).astype(jnp.bfloat16)
    home_rows = jnp.stack([tokens[chosen], scaled_cot]).reshape(2, -1, width)
    both_rows = send_out(home_rows, shift, half, 0)
    token_rows, cot_rows = both_rows[0], both_rows[1]
    partials = jnp.stack(
        [
            jnp.dot(token_rows, wg, preferred_element_type=jnp.float32),
            jnp.dot(token_rows, wu, preferred_element_type=jnp.float32),
            jnp.dot(cot_rows, wd, preferred_element_type=jnp.float32),
        ]
    )
    gate_pre, up_pre, hidden_grad = own_batch(partials, 1)
    gate_sigma = jax.nn.sigmoid(gate_pre)
    hidden = (gate_pre * gate_sigma * up_pre).astype(jnp.bfloat16)
    gate_rows = (hidden_grad * up_pre * gate_sigma * (1.0 + gate_pre * (1.0 - gate_sigma))).astype(
        jnp.bfloat16
    )
    up_rows = (hidden_grad * gate_pre * gate_sigma).astype(jnp.bfloat16)
    hidden_all, gate_all, up_all = both_batches(jnp.stack([hidden, gate_rows, up_rows]), 2)
    partial_value = lax.dot_general(
        hidden_all, wd, CONTRACT_LAST, preferred_element_type=jnp.float32
    ).astype(jnp.bfloat16)
    partial_grad = (
        lax.dot_general(gate_all, wg, CONTRACT_LAST, preferred_element_type=jnp.float32)
        + lax.dot_general(up_all, wu, CONTRACT_LAST, preferred_element_type=jnp.float32)
    ).astype(jnp.bfloat16)
    back = bring_back(jnp.stack([partial_value, partial_grad]), shift, 3)
    back = back.reshape(2, chosen.shape[0], chosen.shape[1], width)
    layer_out = jnp.zeros((tokens.shape[0], width), jnp.float32).at[chosen].add(scales * back[0])
    token_grad = jnp.zeros((tokens.shape[0], width), jnp.float32).at[chosen].add(back[1])
    gate_grad = lax.dot_general(token_rows, gate_all, CONTRACT_FIRST, preferred_element_type=jnp.float32)
    up_grad = lax.dot_general(token_rows, up_all, CONTRACT_FIRST, preferred_element_type=jnp.float32)
    down_grad = lax.dot_general(cot_rows, hidden_all, CONTRACT_FIRST, preferred_element_type=jnp.float32)
    return (
        layer_out.astype(jnp.bfloat16),
        token_grad.astype(jnp.bfloat16),
        gate_grad.astype(jnp.bfloat16)[None],
        up_grad.astype(jnp.bfloat16)[None],
        down_grad.astype(jnp.bfloat16)[None],
    )


def solution(mesh):
    n_dp, n_expert = mesh.devices.shape
    fine = Mesh(mesh.devices.reshape(n_dp, n_expert // SPLIT, SPLIT), ROWS)
    placed = (
        P(ROWS, None),
        P(ROWS, None, None),
        P(ROWS, None, None),
        P(("yx", "col"), "dp", None),
        P(("yx", "col"), "dp", None),
        P(("yx", "col"), "dp", None),
        P(ROWS, None),
    )
    return jax.shard_map(
        shards,
        mesh=fine,
        in_specs=placed,
        out_specs=(
            P(ROWS, None),
            P(ROWS, None),
            P(("yx", "col"), "dp", None),
            P(("yx", "col"), "dp", None),
            P(("yx", "col"), "dp", None),
        ),
        check_vma=False,
    )
```

```python
import jax
import jax.numpy as jnp
from jax import lax
from jax.experimental import pallas as pl
from jax.experimental.pallas import tpu as pltpu
from jax.sharding import Mesh
from jax.sharding import PartitionSpec as P

SPLIT = 8
CHUNKS = 2
ROWS = ("dp", "yx", "col")
MESH_ID = pl.DeviceIdType.MESH
CONTRACT_LAST = (((1,), (1,)), ((), ()))
CONTRACT_FIRST = (((0,), (0,)), ((), ()))


def swap_kernel(src_ref, dst_ref, sems):
    other = 1 - lax.axis_index("dp")
    barrier = pltpu.get_barrier_semaphore()
    pl.semaphore_signal(barrier, 1, device_id={"dp": other}, device_id_type=MESH_ID)
    pl.semaphore_wait(barrier, 1)
    copy = pltpu.make_async_remote_copy(
        src_ref=src_ref,
        dst_ref=dst_ref,
        send_sem=sems.at[0],
        recv_sem=sems.at[1],
        device_id={"dp": other},
        device_id_type=MESH_ID,
    )
    copy.start()
    copy.wait()


def swap_with_partner(x, collective_id):
    size = x.size * x.dtype.itemsize
    return pl.pallas_call(
        swap_kernel,
        out_shape=jax.ShapeDtypeStruct(x.shape, x.dtype),
        in_specs=[pl.BlockSpec(memory_space=pl.ANY)],
        out_specs=pl.BlockSpec(memory_space=pl.ANY),
        scratch_shapes=[pltpu.SemaphoreType.DMA((2,))],
        compiler_params=pltpu.CompilerParams(collective_id=collective_id, has_side_effects=True),
        cost_estimate=pl.CostEstimate(flops=0, bytes_accessed=2 * size, transcendentals=0),
    )(x)


def own_batch(partial, collective_id):
    streams, rows, k = partial.shape
    split = partial.reshape(streams, SPLIT, 2, -1, k)
    traded = swap_with_partner(split[:, :, 1], collective_id)
    return (split[:, :, 0] + traded).reshape(streams, -1, k)


def both_batches(values, collective_id):
    traded = swap_with_partner(values, collective_id)
    streams, rows, k = values.shape
    mine = values.reshape(streams, SPLIT, 1, -1, k)
    theirs = traded.reshape(streams, SPLIT, 1, -1, k)
    return jnp.concatenate([mine, theirs], axis=2).reshape(streams, -1, k)


def expert_chunk(arrived, shift, wg, wu, wd, first_id):
    half = wg.shape[0]
    rolled = jnp.roll(arrived, -shift, axis=-1)
    traded = swap_with_partner(rolled[..., half:], first_id)
    both = jnp.stack([rolled[..., :half], traded], axis=1)
    shared = lax.all_gather(both, "col", axis=1, tiled=False)
    token_rows, cot_rows = shared.reshape(2, -1, half)
    partials = jnp.stack(
        [
            jnp.dot(token_rows, wg, preferred_element_type=jnp.float32),
            jnp.dot(token_rows, wu, preferred_element_type=jnp.float32),
            jnp.dot(cot_rows, wd, preferred_element_type=jnp.float32),
        ]
    )
    gate_pre, up_pre, hidden_grad = own_batch(partials, first_id + 1)
    gate_sigma = jax.nn.sigmoid(gate_pre)
    hidden = (gate_pre * gate_sigma * up_pre).astype(jnp.bfloat16)
    gate_rows = (hidden_grad * up_pre * gate_sigma * (1.0 + gate_pre * (1.0 - gate_sigma))).astype(
        jnp.bfloat16
    )
    up_rows = (hidden_grad * gate_pre * gate_sigma).astype(jnp.bfloat16)
    hidden_all, gate_all, up_all = both_batches(jnp.stack([hidden, gate_rows, up_rows]), first_id + 2)
    partial_value = lax.dot_general(
        hidden_all, wd, CONTRACT_LAST, preferred_element_type=jnp.float32
    ).astype(jnp.bfloat16)
    partial_grad = (
        lax.dot_general(gate_all, wg, CONTRACT_LAST, preferred_element_type=jnp.float32)
        + lax.dot_general(up_all, wu, CONTRACT_LAST, preferred_element_type=jnp.float32)
    ).astype(jnp.bfloat16)
    partial_rows = jnp.stack([partial_value, partial_grad])
    summed = lax.psum_scatter(
        partial_rows.reshape(2, SPLIT, 2, -1, half), "col", scatter_dimension=1, tiled=True
    )[:, 0]
    traded_back = swap_with_partner(summed[:, 1], first_id + 3)
    rows = jnp.roll(jnp.concatenate([summed[:, 0], traded_back], axis=-1), shift, axis=-1)
    grad_terms = jnp.stack(
        [
            lax.dot_general(token_rows, gate_all, CONTRACT_FIRST, preferred_element_type=jnp.float32),
            lax.dot_general(token_rows, up_all, CONTRACT_FIRST, preferred_element_type=jnp.float32),
            lax.dot_general(cot_rows, hidden_all, CONTRACT_FIRST, preferred_element_type=jnp.float32),
        ]
    )
    return rows, grad_terms


def shards(tokens, routes, gate_values, gate_weight, up_weight, down_weight, cotangent):
    width = tokens.shape[1]
    half = gate_weight.shape[1]
    chosen = routes[0]
    scales = gate_values[0][:, :, None]
    shift = lax.axis_index("dp") * half
    wg, wu, wd = gate_weight[0], up_weight[0], down_weight[0]
    scaled_cot = (scales * cotangent[chosen].astype(jnp.float32)).astype(jnp.bfloat16)
    home_rows = jnp.stack([tokens[chosen], scaled_cot]).reshape(2, -1, width)
    arrived = lax.all_to_all(home_rows, "yx", split_axis=1, concat_axis=1, tiled=True)
    cut = arrived.shape[1] // CHUNKS
    outs = [
        expert_chunk(arrived[:, k * cut : (k + 1) * cut], shift, wg, wu, wd, 4 * k)
        for k in range(CHUNKS)
    ]
    rows = jnp.concatenate([o[0] for o in outs], axis=1)
    back = lax.all_to_all(rows, "yx", split_axis=1, concat_axis=1, tiled=True).astype(jnp.float32)
    back = back.reshape(2, chosen.shape[0], chosen.shape[1], width)
    layer_out = jnp.zeros((tokens.shape[0], width), jnp.float32).at[chosen].add(scales * back[0])
    token_grad = jnp.zeros((tokens.shape[0], width), jnp.float32).at[chosen].add(back[1])
    grads = sum(o[1] for o in outs).astype(jnp.bfloat16)
    return (
        layer_out.astype(jnp.bfloat16),
        token_grad.astype(jnp.bfloat16),
        grads[0][None],
        grads[1][None],
        grads[2][None],
    )


def solution(mesh):
    n_dp, n_expert = mesh.devices.shape
    fine = Mesh(mesh.devices.reshape(n_dp, n_expert // SPLIT, SPLIT), ROWS)
    placed = (
        P(ROWS, None),
        P(ROWS, None, None),
        P(ROWS, None, None),
        P(("yx", "col"), "dp", None),
        P(("yx", "col"), "dp", None),
        P(("yx", "col"), "dp", None),
        P(ROWS, None),
    )
    return jax.shard_map(
        shards,
        mesh=fine,
        in_specs=placed,
        out_specs=(
            P(ROWS, None),
            P(ROWS, None),
            P(("yx", "col"), "dp", None),
            P(("yx", "col"), "dp", None),
            P(("yx", "col"), "dp", None),
        ),
        check_vma=False,
    )
```

```python
import jax
import jax.numpy as jnp
from jax import lax
from jax.experimental import pallas as pl
from jax.experimental.pallas import tpu as pltpu
from jax.sharding import Mesh
from jax.sharding import PartitionSpec as P

SPLIT = 8
CHUNKS = 2
ROWS = ("dp", "yx", "col")
MESH_ID = pl.DeviceIdType.MESH
CONTRACT_LAST = (((1,), (1,)), ((), ()))
CONTRACT_FIRST = (((0,), (0,)), ((), ()))


def swap_kernel(src_ref, dst_ref, sems):
    other = 1 - lax.axis_index("dp")
    barrier = pltpu.get_barrier_semaphore()
    pl.semaphore_signal(barrier, 1, device_id={"dp": other}, device_id_type=MESH_ID)
    pl.semaphore_wait(barrier, 1)
    copy = pltpu.make_async_remote_copy(
        src_ref=src_ref,
        dst_ref=dst_ref,
        send_sem=sems.at[0],
        recv_sem=sems.at[1],
        device_id={"dp": other},
        device_id_type=MESH_ID,
    )
    copy.start()
    copy.wait()


def swap_with_partner(x, collective_id):
    size = x.size * x.dtype.itemsize
    return pl.pallas_call(
        swap_kernel,
        out_shape=jax.ShapeDtypeStruct(x.shape, x.dtype),
        in_specs=[pl.BlockSpec(memory_space=pl.ANY)],
        out_specs=pl.BlockSpec(memory_space=pl.ANY),
        scratch_shapes=[pltpu.SemaphoreType.DMA((2,))],
        compiler_params=pltpu.CompilerParams(collective_id=collective_id, has_side_effects=True),
        cost_estimate=pl.CostEstimate(flops=0, bytes_accessed=2 * size, transcendentals=0),
    )(x)


def own_batch(partial, collective_id):
    streams, rows, k = partial.shape
    split = partial.reshape(streams, SPLIT, 2, -1, k)
    traded = swap_with_partner(split[:, :, 1], collective_id)
    return (split[:, :, 0] + traded).reshape(streams, -1, k)


def both_batches(values, collective_id):
    traded = swap_with_partner(values, collective_id)
    streams, rows, k = values.shape
    mine = values.reshape(streams, SPLIT, 1, -1, k)
    theirs = traded.reshape(streams, SPLIT, 1, -1, k)
    return jnp.concatenate([mine, theirs], axis=2).reshape(streams, -1, k)


def expert_chunk(arrived, shift, wg, wu, wd, first_id):
    half = wg.shape[0]
    rolled = jnp.roll(arrived, -shift, axis=-1)
    traded = swap_with_partner(rolled[..., half:], first_id)
    both = jnp.stack([rolled[..., :half], traded], axis=1)
    shared = lax.all_gather(both, "col", axis=1, tiled=False)
    token_rows, cot_rows = shared.reshape(2, -1, half)
    partials = jnp.stack(
        [
            jnp.dot(token_rows, wg, preferred_element_type=jnp.float32),
            jnp.dot(token_rows, wu, preferred_element_type=jnp.float32),
            jnp.dot(cot_rows, wd, preferred_element_type=jnp.float32),
        ]
    )
    gate_pre, up_pre, hidden_grad = own_batch(partials, first_id + 1)
    gate_sigma = jax.nn.sigmoid(gate_pre)
    hidden = (gate_pre * gate_sigma * up_pre).astype(jnp.bfloat16)
    gate_rows = (hidden_grad * up_pre * gate_sigma * (1.0 + gate_pre * (1.0 - gate_sigma))).astype(
        jnp.bfloat16
    )
    up_rows = (hidden_grad * gate_pre * gate_sigma).astype(jnp.bfloat16)
    hidden_all, gate_all, up_all = both_batches(jnp.stack([hidden, gate_rows, up_rows]), first_id + 2)
    partial_value = lax.dot_general(
        hidden_all, wd, CONTRACT_LAST, preferred_element_type=jnp.float32
    ).astype(jnp.bfloat16)
    partial_grad = (
        lax.dot_general(gate_all, wg, CONTRACT_LAST, preferred_element_type=jnp.float32)
        + lax.dot_general(up_all, wu, CONTRACT_LAST, preferred_element_type=jnp.float32)
    ).astype(jnp.bfloat16)
    partial_rows = jnp.stack([partial_value, partial_grad])
    summed = lax.psum_scatter(
        partial_rows.reshape(2, SPLIT, 2, -1, half), "col", scatter_dimension=1, tiled=True
    )[:, 0]
    traded_back = swap_with_partner(summed[:, 1], first_id + 3)
    rows = jnp.roll(jnp.concatenate([summed[:, 0], traded_back], axis=-1), shift, axis=-1)
    grad_terms = jnp.stack(
        [
            lax.dot_general(token_rows, gate_all, CONTRACT_FIRST, preferred_element_type=jnp.float32),
            lax.dot_general(token_rows, up_all, CONTRACT_FIRST, preferred_element_type=jnp.float32),
            lax.dot_general(cot_rows, hidden_all, CONTRACT_FIRST, preferred_element_type=jnp.float32),
        ]
    )
    return rows, grad_terms


def shards(tokens, routes, gate_values, gate_weight, up_weight, down_weight, cotangent):
    width = tokens.shape[1]
    half = gate_weight.shape[1]
    chosen = routes[0]
    scales = gate_values[0][:, :, None]
    shift = lax.axis_index("dp") * half
    wg, wu, wd = gate_weight[0], up_weight[0], down_weight[0]
    scaled_cot = (scales * cotangent[chosen].astype(jnp.float32)).astype(jnp.bfloat16)
    home_rows = jnp.stack([tokens[chosen], scaled_cot])
    experts, slots = chosen.shape
    cut = slots // CHUNKS
    backs = []
    grads = 0.0
    for k in range(CHUNKS):
        chunk = home_rows[:, :, k * cut : (k + 1) * cut].reshape(2, -1, width)
        arrived = lax.all_to_all(chunk, "yx", split_axis=1, concat_axis=1, tiled=True)
        rows, grad_terms = expert_chunk(arrived, shift, wg, wu, wd, 4 * k)
        back = lax.all_to_all(rows, "yx", split_axis=1, concat_axis=1, tiled=True)
        backs.append(back.reshape(2, experts, cut, width))
        grads = grads + grad_terms
    back = jnp.concatenate(backs, axis=2).astype(jnp.float32)
    grads = grads.astype(jnp.bfloat16)
    layer_out = jnp.zeros((tokens.shape[0], width), jnp.float32).at[chosen].add(scales * back[0])
    token_grad = jnp.zeros((tokens.shape[0], width), jnp.float32).at[chosen].add(back[1])
    return (
        layer_out.astype(jnp.bfloat16),
        token_grad.astype(jnp.bfloat16),
        grads[0][None],
        grads[1][None],
        grads[2][None],
    )


def solution(mesh):
    n_dp, n_expert = mesh.devices.shape
    fine = Mesh(mesh.devices.reshape(n_dp, n_expert // SPLIT, SPLIT), ROWS)
    placed = (
        P(ROWS, None),
        P(ROWS, None, None),
        P(ROWS, None, None),
        P(("yx", "col"), "dp", None),
        P(("yx", "col"), "dp", None),
        P(("yx", "col"), "dp", None),
        P(ROWS, None),
    )
    return jax.shard_map(
        shards,
        mesh=fine,
        in_specs=placed,
        out_specs=(
            P(ROWS, None),
            P(ROWS, None),
            P(("yx", "col"), "dp", None),
            P(("yx", "col"), "dp", None),
            P(("yx", "col"), "dp", None),
        ),
        check_vma=False,
    )
```

```python
import jax
import jax.numpy as jnp
from jax import lax
from jax.experimental import pallas as pl
from jax.experimental.pallas import tpu as pltpu
from jax.sharding import Mesh
from jax.sharding import PartitionSpec as P

SPLIT = 8
CHUNKS = 2
ROWS = ("dp", "yx", "col")
MESH_ID = pl.DeviceIdType.MESH
CONTRACT_LAST = (((1,), (1,)), ((), ()))
CONTRACT_FIRST = (((0,), (0,)), ((), ()))


def swap_kernel(src_ref, dst_ref, sems):
    other = 1 - lax.axis_index("dp")
    barrier = pltpu.get_barrier_semaphore()
    pl.semaphore_signal(barrier, 1, device_id={"dp": other}, device_id_type=MESH_ID)
    pl.semaphore_wait(barrier, 1)
    copy = pltpu.make_async_remote_copy(
        src_ref=src_ref,
        dst_ref=dst_ref,
        send_sem=sems.at[0],
        recv_sem=sems.at[1],
        device_id={"dp": other},
        device_id_type=MESH_ID,
    )
    copy.start()
    copy.wait()


def swap_with_partner(x, collective_id):
    size = x.size * x.dtype.itemsize
    return pl.pallas_call(
        swap_kernel,
        out_shape=jax.ShapeDtypeStruct(x.shape, x.dtype),
        in_specs=[pl.BlockSpec(memory_space=pl.ANY)],
        out_specs=pl.BlockSpec(memory_space=pl.ANY),
        scratch_shapes=[pltpu.SemaphoreType.DMA((2,))],
        compiler_params=pltpu.CompilerParams(collective_id=collective_id, has_side_effects=True),
        cost_estimate=pl.CostEstimate(flops=0, bytes_accessed=2 * size, transcendentals=0),
    )(x)


def own_batch(partial, collective_id):
    streams, rows, k = partial.shape
    split = partial.reshape(streams, SPLIT, 2, -1, k)
    traded = swap_with_partner(split[:, :, 1].astype(jnp.bfloat16), collective_id)
    return (split[:, :, 0] + traded.astype(jnp.float32)).reshape(streams, -1, k)


def both_batches(values, collective_id):
    traded = swap_with_partner(values, collective_id)
    streams, rows, k = values.shape
    mine = values.reshape(streams, SPLIT, 1, -1, k)
    theirs = traded.reshape(streams, SPLIT, 1, -1, k)
    return jnp.concatenate([mine, theirs], axis=2).reshape(streams, -1, k)


def trade_halves(arrived, shift, half, collective_id):
    rolled = jnp.roll(arrived, -shift, axis=-1)
    traded = swap_with_partner(rolled[..., half:], collective_id)
    return jnp.stack([rolled[..., :half], traded], axis=1)


def expert_chunk(arrived, shift, wg, wu, wd, first_id):
    half = wg.shape[0]
    shared = lax.all_gather(arrived, "col", axis=1, tiled=False)
    token_rows, cot_rows = shared.reshape(2, -1, half)
    partials = jnp.stack(
        [
            jnp.dot(token_rows, wg, preferred_element_type=jnp.float32),
            jnp.dot(token_rows, wu, preferred_element_type=jnp.float32),
            jnp.dot(cot_rows, wd, preferred_element_type=jnp.float32),
        ]
    )
    gate_pre, up_pre, hidden_grad = own_batch(partials, first_id + 1)
    gate_sigma = jax.nn.sigmoid(gate_pre)
    hidden = (gate_pre * gate_sigma * up_pre).astype(jnp.bfloat16)
    gate_rows = (hidden_grad * up_pre * gate_sigma * (1.0 + gate_pre * (1.0 - gate_sigma))).astype(
        jnp.bfloat16
    )
    up_rows = (hidden_grad * gate_pre * gate_sigma).astype(jnp.bfloat16)
    hidden_all, gate_all, up_all = both_batches(jnp.stack([hidden, gate_rows, up_rows]), first_id + 2)
    partial_value = lax.dot_general(
        hidden_all, wd, CONTRACT_LAST, preferred_element_type=jnp.float32
    ).astype(jnp.bfloat16)
    partial_grad = (
        lax.dot_general(gate_all, wg, CONTRACT_LAST, preferred_element_type=jnp.float32)
        + lax.dot_general(up_all, wu, CONTRACT_LAST, preferred_element_type=jnp.float32)
    ).astype(jnp.bfloat16)
    partial_rows = jnp.stack([partial_value, partial_grad])
    summed = lax.psum_scatter(
        partial_rows.reshape(2, SPLIT, 2, -1, half), "col", scatter_dimension=1, tiled=True
    )[:, 0]
    traded_back = swap_with_partner(summed[:, 1], first_id + 3)
    rows = jnp.roll(jnp.concatenate([summed[:, 0], traded_back], axis=-1), shift, axis=-1)
    grad_terms = jnp.stack(
        [
            lax.dot_general(token_rows, gate_all, CONTRACT_FIRST, preferred_element_type=jnp.float32),
            lax.dot_general(token_rows, up_all, CONTRACT_FIRST, preferred_element_type=jnp.float32),
            lax.dot_general(cot_rows, hidden_all, CONTRACT_FIRST, preferred_element_type=jnp.float32),
        ]
    )
    return rows, grad_terms


def shards(tokens, routes, gate_values, gate_weight, up_weight, down_weight, cotangent):
    width = tokens.shape[1]
    half = gate_weight.shape[1]
    chosen = routes[0]
    scales = gate_values[0][:, :, None]
    shift = lax.axis_index("dp") * half
    wg, wu, wd = gate_weight[0], up_weight[0], down_weight[0]
    scaled_cot = (scales * cotangent[chosen].astype(jnp.float32)).astype(jnp.bfloat16)
    home_rows = jnp.stack([tokens[chosen], scaled_cot])
    experts, slots = chosen.shape
    cut = slots // CHUNKS
    backs = []
    grads = 0.0
    traded = []
    for k in range(CHUNKS):
        chunk = home_rows[:, :, k * cut : (k + 1) * cut].reshape(2, -1, width)
        if traded:
            chunk, _ = lax.optimization_barrier((chunk, traded[-1]))
        arrived = lax.all_to_all(chunk, "yx", split_axis=1, concat_axis=1, tiled=True)
        traded.append(trade_halves(arrived, shift, half, 4 * k))
    for k in range(CHUNKS):
        rows, grad_terms = expert_chunk(traded[k], shift, wg, wu, wd, 4 * k)
        back = lax.all_to_all(rows, "yx", split_axis=1, concat_axis=1, tiled=True)
        backs.append(back.reshape(2, experts, cut, width))
        grads = grads + grad_terms
    back = jnp.concatenate(backs, axis=2).astype(jnp.float32)
    grads = grads.astype(jnp.bfloat16)
    layer_out = jnp.zeros((tokens.shape[0], width), jnp.float32).at[chosen].add(scales * back[0])
    token_grad = jnp.zeros((tokens.shape[0], width), jnp.float32).at[chosen].add(back[1])
    return (
        layer_out.astype(jnp.bfloat16),
        token_grad.astype(jnp.bfloat16),
        grads[0][None],
        grads[1][None],
        grads[2][None],
    )


def solution(mesh):
    n_dp, n_expert = mesh.devices.shape
    fine = Mesh(mesh.devices.reshape(n_dp, n_expert // SPLIT, SPLIT), ROWS)
    placed = (
        P(ROWS, None),
        P(ROWS, None, None),
        P(ROWS, None, None),
        P(("yx", "col"), "dp", None),
        P(("yx", "col"), "dp", None),
        P(("yx", "col"), "dp", None),
        P(ROWS, None),
    )
    return jax.shard_map(
        shards,
        mesh=fine,
        in_specs=placed,
        out_specs=(
            P(ROWS, None),
            P(ROWS, None),
            P(("yx", "col"), "dp", None),
            P(("yx", "col"), "dp", None),
            P(("yx", "col"), "dp", None),
        ),
        check_vma=False,
    )
```

```python
import jax
import jax.numpy as jnp
from jax import lax
from jax.experimental import pallas as pl
from jax.experimental.pallas import tpu as pltpu
from jax.sharding import Mesh
from jax.sharding import PartitionSpec as P

SPLIT = 8
CHUNKS = 2
ROWS = ("dp", "yx", "col")
MESH_ID = pl.DeviceIdType.MESH
CONTRACT_LAST = (((1,), (1,)), ((), ()))
CONTRACT_FIRST = (((0,), (0,)), ((), ()))


def swap_kernel(src_ref, dst_ref, sems):
    other = 1 - lax.axis_index("dp")
    barrier = pltpu.get_barrier_semaphore()
    pl.semaphore_signal(barrier, 1, device_id={"dp": other}, device_id_type=MESH_ID)
    pl.semaphore_wait(barrier, 1)
    copy = pltpu.make_async_remote_copy(
        src_ref=src_ref,
        dst_ref=dst_ref,
        send_sem=sems.at[0],
        recv_sem=sems.at[1],
        device_id={"dp": other},
        device_id_type=MESH_ID,
    )
    copy.start()
    copy.wait()


def swap_with_partner(x, collective_id):
    size = x.size * x.dtype.itemsize
    return pl.pallas_call(
        swap_kernel,
        out_shape=jax.ShapeDtypeStruct(x.shape, x.dtype),
        in_specs=[pl.BlockSpec(memory_space=pl.ANY)],
        out_specs=pl.BlockSpec(memory_space=pl.ANY),
        scratch_shapes=[pltpu.SemaphoreType.DMA((2,))],
        compiler_params=pltpu.CompilerParams(collective_id=collective_id, has_side_effects=True),
        cost_estimate=pl.CostEstimate(flops=0, bytes_accessed=2 * size, transcendentals=0),
    )(x)


def own_batch(partial, collective_id):
    streams, rows, k = partial.shape
    split = partial.reshape(streams, SPLIT, 2, -1, k)
    traded = swap_with_partner(split[:, :, 1].astype(jnp.bfloat16), collective_id)
    return (split[:, :, 0] + traded.astype(jnp.float32)).reshape(streams, -1, k)


def both_batches(values, collective_id):
    traded = swap_with_partner(values, collective_id)
    streams, rows, k = values.shape
    mine = values.reshape(streams, SPLIT, 1, -1, k)
    theirs = traded.reshape(streams, SPLIT, 1, -1, k)
    return jnp.concatenate([mine, theirs], axis=2).reshape(streams, -1, k)


def trade_halves(arrived, shift, half, collective_id):
    rolled = jnp.roll(arrived, -shift, axis=-1)
    traded = swap_with_partner(rolled[..., half:], collective_id)
    return jnp.stack([rolled[..., :half], traded], axis=1)


def expert_chunk(arrived, shift, wg, wu, wd, first_id):
    half = wg.shape[0]
    shared = lax.all_gather(arrived, "col", axis=1, tiled=False)
    token_rows, cot_rows = shared.reshape(2, -1, half)
    partials = jnp.stack(
        [
            jnp.dot(token_rows, wg, preferred_element_type=jnp.float32),
            jnp.dot(token_rows, wu, preferred_element_type=jnp.float32),
            jnp.dot(cot_rows, wd, preferred_element_type=jnp.float32),
        ]
    )
    gate_pre, up_pre, hidden_grad = own_batch(partials, first_id + 1)
    gate_sigma = jax.nn.sigmoid(gate_pre)
    hidden = (gate_pre * gate_sigma * up_pre).astype(jnp.bfloat16)
    gate_rows = (hidden_grad * up_pre * gate_sigma * (1.0 + gate_pre * (1.0 - gate_sigma))).astype(
        jnp.bfloat16
    )
    up_rows = (hidden_grad * gate_pre * gate_sigma).astype(jnp.bfloat16)
    hidden_all, gate_all, up_all = both_batches(jnp.stack([hidden, gate_rows, up_rows]), first_id + 2)
    partial_value = lax.dot_general(
        hidden_all, wd, CONTRACT_LAST, preferred_element_type=jnp.float32
    ).astype(jnp.bfloat16)
    partial_grad = (
        lax.dot_general(gate_all, wg, CONTRACT_LAST, preferred_element_type=jnp.float32)
        + lax.dot_general(up_all, wu, CONTRACT_LAST, preferred_element_type=jnp.float32)
    ).astype(jnp.bfloat16)
    partial_rows = jnp.stack([partial_value, partial_grad])
    grad_terms = jnp.stack(
        [
            lax.dot_general(token_rows, gate_all, CONTRACT_FIRST, preferred_element_type=jnp.float32),
            lax.dot_general(token_rows, up_all, CONTRACT_FIRST, preferred_element_type=jnp.float32),
            lax.dot_general(cot_rows, hidden_all, CONTRACT_FIRST, preferred_element_type=jnp.float32),
        ]
    )
    return partial_rows, grad_terms


def bring_back(partial_rows, shift, collective_id):
    half = partial_rows.shape[-1]
    summed = lax.psum_scatter(
        partial_rows.reshape(2, SPLIT, 2, -1, half), "col", scatter_dimension=1, tiled=True
    )[:, 0]
    traded_back = swap_with_partner(summed[:, 1], collective_id)
    return jnp.roll(jnp.concatenate([summed[:, 0], traded_back], axis=-1), shift, axis=-1)


def shards(tokens, routes, gate_values, gate_weight, up_weight, down_weight, cotangent):
    width = tokens.shape[1]
    half = gate_weight.shape[1]
    chosen = routes[0]
    scales = gate_values[0][:, :, None]
    shift = lax.axis_index("dp") * half
    wg, wu, wd = gate_weight[0], up_weight[0], down_weight[0]
    scaled_cot = (scales * cotangent[chosen].astype(jnp.float32)).astype(jnp.bfloat16)
    home_rows = jnp.stack([tokens[chosen], scaled_cot])
    experts, slots = chosen.shape
    cut = slots // CHUNKS
    backs = []
    grads = 0.0
    traded = []
    for k in range(CHUNKS):
        chunk = home_rows[:, :, k * cut : (k + 1) * cut].reshape(2, -1, width)
        if traded:
            chunk, _ = lax.optimization_barrier((chunk, traded[-1]))
        arrived = lax.all_to_all(chunk, "yx", split_axis=1, concat_axis=1, tiled=True)
        traded.append(trade_halves(arrived, shift, half, 4 * k))
    computed = [expert_chunk(traded[k], shift, wg, wu, wd, 4 * k) for k in range(CHUNKS)]
    grads = sum(c[1] for c in computed).astype(jnp.bfloat16)
    layer_out = jnp.zeros((tokens.shape[0], width), jnp.float32)
    token_grad = jnp.zeros((tokens.shape[0], width), jnp.float32)
    for k in range(CHUNKS):
        partial_rows = computed[k][0]
        if k == CHUNKS - 1:
            partial_rows, grads = lax.optimization_barrier((partial_rows, grads))
        rows = bring_back(partial_rows, shift, 4 * k + 3)
        back = lax.all_to_all(rows, "yx", split_axis=1, concat_axis=1, tiled=True)
        back = back.astype(jnp.float32).reshape(2, experts, cut, width)
        taken = chosen[:, k * cut : (k + 1) * cut]
        layer_out = layer_out.at[taken].add(scales[:, k * cut : (k + 1) * cut] * back[0])
        token_grad = token_grad.at[taken].add(back[1])
    return (
        layer_out.astype(jnp.bfloat16),
        token_grad.astype(jnp.bfloat16),
        grads[0][None],
        grads[1][None],
        grads[2][None],
    )


def solution(mesh):
    n_dp, n_expert = mesh.devices.shape
    fine = Mesh(mesh.devices.reshape(n_dp, n_expert // SPLIT, SPLIT), ROWS)
    placed = (
        P(ROWS, None),
        P(ROWS, None, None),
        P(ROWS, None, None),
        P(("yx", "col"), "dp", None),
        P(("yx", "col"), "dp", None),
        P(("yx", "col"), "dp", None),
        P(ROWS, None),
    )
    return jax.shard_map(
        shards,
        mesh=fine,
        in_specs=placed,
        out_specs=(
            P(ROWS, None),
            P(ROWS, None),
            P(("yx", "col"), "dp", None),
            P(("yx", "col"), "dp", None),
            P(("yx", "col"), "dp", None),
        ),
        check_vma=False,
    )
```

```python
import jax
import jax.numpy as jnp
from jax import lax
from jax.experimental import pallas as pl
from jax.experimental.pallas import tpu as pltpu
from jax.sharding import Mesh
from jax.sharding import PartitionSpec as P

SPLIT = 8
CHUNKS = 2
ROWS = ("dp", "yx", "col")
MESH_ID = pl.DeviceIdType.MESH
CONTRACT_LAST = (((1,), (1,)), ((), ()))
CONTRACT_FIRST = (((0,), (0,)), ((), ()))


def swap_kernel(src_ref, dst_ref, sems):
    other = 1 - lax.axis_index("dp")
    barrier = pltpu.get_barrier_semaphore()
    pl.semaphore_signal(barrier, 1, device_id={"dp": other}, device_id_type=MESH_ID)
    pl.semaphore_wait(barrier, 1)
    copy = pltpu.make_async_remote_copy(
        src_ref=src_ref,
        dst_ref=dst_ref,
        send_sem=sems.at[0],
        recv_sem=sems.at[1],
        device_id={"dp": other},
        device_id_type=MESH_ID,
    )
    copy.start()
    copy.wait()


def swap_with_partner(x, collective_id):
    size = x.size * x.dtype.itemsize
    return pl.pallas_call(
        swap_kernel,
        out_shape=jax.ShapeDtypeStruct(x.shape, x.dtype),
        in_specs=[pl.BlockSpec(memory_space=pl.ANY)],
        out_specs=pl.BlockSpec(memory_space=pl.ANY),
        scratch_shapes=[pltpu.SemaphoreType.DMA((2,))],
        compiler_params=pltpu.CompilerParams(collective_id=collective_id, has_side_effects=True),
        cost_estimate=pl.CostEstimate(flops=0, bytes_accessed=2 * size, transcendentals=0),
    )(x)


def own_batch(partial, collective_id):
    streams, rows, k = partial.shape
    split = partial.reshape(streams, SPLIT, 2, -1, k)
    traded = swap_with_partner(split[:, :, 1].astype(jnp.bfloat16), collective_id)
    return (split[:, :, 0] + traded.astype(jnp.float32)).reshape(streams, -1, k)


def both_batches(values, collective_id):
    traded = swap_with_partner(values, collective_id)
    streams, rows, k = values.shape
    mine = values.reshape(streams, SPLIT, 1, -1, k)
    theirs = traded.reshape(streams, SPLIT, 1, -1, k)
    return jnp.concatenate([mine, theirs], axis=2).reshape(streams, -1, k)


def trade_halves(arrived, shift, half, collective_id):
    rolled = jnp.roll(arrived, -shift, axis=-1)
    traded = swap_with_partner(rolled[..., half:], collective_id)
    return jnp.stack([rolled[..., :half], traded], axis=1)


def expert_chunk(arrived, shift, wg, wu, wd, first_id):
    half = wg.shape[0]
    shared = lax.all_gather(arrived, "col", axis=1, tiled=False)
    token_rows, cot_rows = shared.reshape(2, -1, half)
    partials = jnp.stack(
        [
            jnp.dot(token_rows, wg, preferred_element_type=jnp.float32),
            jnp.dot(token_rows, wu, preferred_element_type=jnp.float32),
            jnp.dot(cot_rows, wd, preferred_element_type=jnp.float32),
        ]
    )
    gate_pre, up_pre, hidden_grad = own_batch(partials, first_id + 1)
    gate_sigma = jax.nn.sigmoid(gate_pre)
    hidden = (gate_pre * gate_sigma * up_pre).astype(jnp.bfloat16)
    gate_rows = (hidden_grad * up_pre * gate_sigma * (1.0 + gate_pre * (1.0 - gate_sigma))).astype(
        jnp.bfloat16
    )
    up_rows = (hidden_grad * gate_pre * gate_sigma).astype(jnp.bfloat16)
    hidden_all, gate_all, up_all = both_batches(jnp.stack([hidden, gate_rows, up_rows]), first_id + 2)
    partial_value = lax.dot_general(
        hidden_all, wd, CONTRACT_LAST, preferred_element_type=jnp.float32
    ).astype(jnp.bfloat16)
    partial_grad = (
        lax.dot_general(gate_all, wg, CONTRACT_LAST, preferred_element_type=jnp.float32)
        + lax.dot_general(up_all, wu, CONTRACT_LAST, preferred_element_type=jnp.float32)
    ).astype(jnp.bfloat16)
    partial_rows = jnp.stack([partial_value, partial_grad])
    grad_terms = jnp.stack(
        [
            lax.dot_general(token_rows, gate_all, CONTRACT_FIRST, preferred_element_type=jnp.float32),
            lax.dot_general(token_rows, up_all, CONTRACT_FIRST, preferred_element_type=jnp.float32),
            lax.dot_general(cot_rows, hidden_all, CONTRACT_FIRST, preferred_element_type=jnp.float32),
        ]
    )
    return partial_rows, grad_terms


def bring_back(partial_rows, shift, collective_id, grads=None):
    half = partial_rows.shape[-1]
    summed = lax.psum_scatter(
        partial_rows.reshape(2, SPLIT, 2, -1, half), "col", scatter_dimension=1, tiled=True
    )[:, 0]
    if grads is not None:
        summed, grads = lax.optimization_barrier((summed, grads))
    traded_back = swap_with_partner(summed[:, 1], collective_id)
    rows = jnp.roll(jnp.concatenate([summed[:, 0], traded_back], axis=-1), shift, axis=-1)
    return rows, grads


def shards(tokens, routes, gate_values, gate_weight, up_weight, down_weight, cotangent):
    width = tokens.shape[1]
    half = gate_weight.shape[1]
    chosen = routes[0]
    scales = gate_values[0][:, :, None]
    shift = lax.axis_index("dp") * half
    wg, wu, wd = gate_weight[0], up_weight[0], down_weight[0]
    experts, slots = chosen.shape
    cut = slots // CHUNKS
    traded = []
    for k in range(CHUNKS):
        taken = chosen[:, k * cut : (k + 1) * cut]
        gains = scales[:, k * cut : (k + 1) * cut]
        scaled_cot = (gains * cotangent[taken].astype(jnp.float32)).astype(jnp.bfloat16)
        chunk = jnp.stack([tokens[taken], scaled_cot]).reshape(2, -1, width)
        if traded:
            chunk, _ = lax.optimization_barrier((chunk, traded[-1]))
        arrived = lax.all_to_all(chunk, "yx", split_axis=1, concat_axis=1, tiled=True)
        traded.append(trade_halves(arrived, shift, half, 4 * k))
    computed = [expert_chunk(traded[k], shift, wg, wu, wd, 4 * k) for k in range(CHUNKS)]
    grads = sum(c[1] for c in computed)
    backs = []
    for k in range(CHUNKS):
        last = k == CHUNKS - 1
        rows, finished = bring_back(computed[k][0], shift, 4 * k + 3, grads if last else None)
        if last:
            grads = finished
        back = lax.all_to_all(rows, "yx", split_axis=1, concat_axis=1, tiled=True)
        backs.append(back.reshape(2, experts, cut, width))
    back = jnp.concatenate(backs, axis=2).astype(jnp.float32)
    grads = grads.astype(jnp.bfloat16)
    layer_out = jnp.zeros((tokens.shape[0], width), jnp.float32).at[chosen].add(scales * back[0])
    token_grad = jnp.zeros((tokens.shape[0], width), jnp.float32).at[chosen].add(back[1])
    return (
        layer_out.astype(jnp.bfloat16),
        token_grad.astype(jnp.bfloat16),
        grads[0][None],
        grads[1][None],
        grads[2][None],
    )


def solution(mesh):
    n_dp, n_expert = mesh.devices.shape
    fine = Mesh(mesh.devices.reshape(n_dp, n_expert // SPLIT, SPLIT), ROWS)
    placed = (
        P(ROWS, None),
        P(ROWS, None, None),
        P(ROWS, None, None),
        P(("yx", "col"), "dp", None),
        P(("yx", "col"), "dp", None),
        P(("yx", "col"), "dp", None),
        P(ROWS, None),
    )
    return jax.shard_map(
        shards,
        mesh=fine,
        in_specs=placed,
        out_specs=(
            P(ROWS, None),
            P(ROWS, None),
            P(("yx", "col"), "dp", None),
            P(("yx", "col"), "dp", None),
            P(("yx", "col"), "dp", None),
        ),
        check_vma=False,
    )
```

```python
import jax
import jax.numpy as jnp
from jax import lax
from jax.experimental import pallas as pl
from jax.experimental.pallas import tpu as pltpu
from jax.sharding import Mesh
from jax.sharding import PartitionSpec as P

SPLIT = 8
CHUNKS = 2
ROWS = ("dp", "yx", "col")
MESH_ID = pl.DeviceIdType.MESH
CONTRACT_LAST = (((1,), (1,)), ((), ()))
CONTRACT_FIRST = (((0,), (0,)), ((), ()))


def swap_kernel(src_ref, dst_ref, sems):
    other = 1 - lax.axis_index("dp")
    barrier = pltpu.get_barrier_semaphore()
    pl.semaphore_signal(barrier, 1, device_id={"dp": other}, device_id_type=MESH_ID)
    pl.semaphore_wait(barrier, 1)
    copy = pltpu.make_async_remote_copy(
        src_ref=src_ref,
        dst_ref=dst_ref,
        send_sem=sems.at[0],
        recv_sem=sems.at[1],
        device_id={"dp": other},
        device_id_type=MESH_ID,
    )
    copy.start()
    copy.wait()


def swap_with_partner(x, collective_id):
    size = x.size * x.dtype.itemsize
    return pl.pallas_call(
        swap_kernel,
        out_shape=jax.ShapeDtypeStruct(x.shape, x.dtype),
        in_specs=[pl.BlockSpec(memory_space=pl.ANY)],
        out_specs=pl.BlockSpec(memory_space=pl.ANY),
        scratch_shapes=[pltpu.SemaphoreType.DMA((2,))],
        compiler_params=pltpu.CompilerParams(collective_id=collective_id, has_side_effects=True),
        cost_estimate=pl.CostEstimate(flops=0, bytes_accessed=2 * size, transcendentals=0),
    )(x)


def own_batch(partial, collective_id):
    streams, rows, k = partial.shape
    split = partial.reshape(streams, SPLIT, 2, -1, k)
    traded = swap_with_partner(split[:, :, 1].astype(jnp.bfloat16), collective_id)
    return (split[:, :, 0] + traded.astype(jnp.float32)).reshape(streams, -1, k)


def both_batches(values, collective_id):
    traded = swap_with_partner(values, collective_id)
    streams, rows, k = values.shape
    mine = values.reshape(streams, SPLIT, 1, -1, k)
    theirs = traded.reshape(streams, SPLIT, 1, -1, k)
    return jnp.concatenate([mine, theirs], axis=2).reshape(streams, -1, k)


def trade_halves(arrived, shift, half, collective_id):
    rolled = jnp.roll(arrived, -shift, axis=-1)
    traded = swap_with_partner(rolled[..., half:], collective_id)
    return jnp.stack([rolled[..., :half], traded], axis=1)


def expert_chunk(arrived, shift, wg, wu, wd, first_id):
    half = wg.shape[0]
    shared = lax.all_gather(arrived, "col", axis=1, tiled=False)
    token_rows, cot_rows = shared.reshape(2, -1, half)
    partials = jnp.stack(
        [
            jnp.dot(token_rows, wg, preferred_element_type=jnp.float32),
            jnp.dot(token_rows, wu, preferred_element_type=jnp.float32),
            jnp.dot(cot_rows, wd, preferred_element_type=jnp.float32),
        ]
    )
    gate_pre, up_pre, hidden_grad = own_batch(partials, first_id + 1)
    gate_sigma = jax.nn.sigmoid(gate_pre)
    hidden = (gate_pre * gate_sigma * up_pre).astype(jnp.bfloat16)
    gate_rows = (hidden_grad * up_pre * gate_sigma * (1.0 + gate_pre * (1.0 - gate_sigma))).astype(
        jnp.bfloat16
    )
    up_rows = (hidden_grad * gate_pre * gate_sigma).astype(jnp.bfloat16)
    hidden_all, gate_all, up_all = both_batches(jnp.stack([hidden, gate_rows, up_rows]), first_id + 2)
    partial_value = lax.dot_general(
        hidden_all, wd, CONTRACT_LAST, preferred_element_type=jnp.float32
    ).astype(jnp.bfloat16)
    partial_grad = (
        lax.dot_general(gate_all, wg, CONTRACT_LAST, preferred_element_type=jnp.float32)
        + lax.dot_general(up_all, wu, CONTRACT_LAST, preferred_element_type=jnp.float32)
    ).astype(jnp.bfloat16)
    partial_rows = jnp.stack([partial_value, partial_grad])
    grad_terms = jnp.stack(
        [
            lax.dot_general(token_rows, gate_all, CONTRACT_FIRST, preferred_element_type=jnp.float32),
            lax.dot_general(token_rows, up_all, CONTRACT_FIRST, preferred_element_type=jnp.float32),
            lax.dot_general(cot_rows, hidden_all, CONTRACT_FIRST, preferred_element_type=jnp.float32),
        ]
    )
    return partial_rows, grad_terms


def bring_back(partial_rows, shift, collective_id, grads=None):
    half = partial_rows.shape[-1]
    summed = lax.psum_scatter(
        partial_rows.reshape(2, SPLIT, 2, -1, half), "col", scatter_dimension=1, tiled=True
    )[:, 0]
    if grads is not None:
        summed, grads = lax.optimization_barrier((summed, grads))
    traded_back = swap_with_partner(summed[:, 1], collective_id)
    rows = jnp.roll(jnp.concatenate([summed[:, 0], traded_back], axis=-1), shift, axis=-1)
    return rows, grads


def shards(tokens, routes, gate_values, gate_weight, up_weight, down_weight, cotangent):
    width = tokens.shape[1]
    half = gate_weight.shape[1]
    chosen = routes[0]
    scales = gate_values[0][:, :, None]
    shift = lax.axis_index("dp") * half
    wg, wu, wd = gate_weight[0], up_weight[0], down_weight[0]
    experts, slots = chosen.shape
    cut = slots // CHUNKS
    traded = []
    for k in range(CHUNKS):
        taken = chosen[:, k * cut : (k + 1) * cut]
        gains = scales[:, k * cut : (k + 1) * cut]
        scaled_cot = (gains * cotangent[taken].astype(jnp.float32)).astype(jnp.bfloat16)
        chunk = jnp.stack([tokens[taken], scaled_cot]).reshape(2, -1, width)
        if traded:
            chunk, _ = lax.optimization_barrier((chunk, traded[-1]))
        arrived = lax.all_to_all(chunk, "yx", split_axis=1, concat_axis=1, tiled=True)
        traded.append(trade_halves(arrived, shift, half, 4 * k))
    computed = [expert_chunk(traded[k], shift, wg, wu, wd, 4 * k) for k in range(CHUNKS)]
    grads = sum(c[1] for c in computed)
    layer_out = jnp.zeros((tokens.shape[0], width), jnp.float32)
    token_grad = jnp.zeros((tokens.shape[0], width), jnp.float32)
    for k in range(CHUNKS):
        last = k == CHUNKS - 1
        rows, finished = bring_back(computed[k][0], shift, 4 * k + 3, grads if last else None)
        if last:
            grads = finished
        back = lax.all_to_all(rows, "yx", split_axis=1, concat_axis=1, tiled=True)
        back = back.astype(jnp.float32).reshape(2, experts, cut, width)
        taken = chosen[:, k * cut : (k + 1) * cut]
        layer_out = layer_out.at[taken].add(scales[:, k * cut : (k + 1) * cut] * back[0])
        token_grad = token_grad.at[taken].add(back[1])
    grads = grads.astype(jnp.bfloat16)
    return (
        layer_out.astype(jnp.bfloat16),
        token_grad.astype(jnp.bfloat16),
        grads[0][None],
        grads[1][None],
        grads[2][None],
    )


def solution(mesh):
    n_dp, n_expert = mesh.devices.shape
    fine = Mesh(mesh.devices.reshape(n_dp, n_expert // SPLIT, SPLIT), ROWS)
    placed = (
        P(ROWS, None),
        P(ROWS, None, None),
        P(ROWS, None, None),
        P(("yx", "col"), "dp", None),
        P(("yx", "col"), "dp", None),
        P(("yx", "col"), "dp", None),
        P(ROWS, None),
    )
    return jax.shard_map(
        shards,
        mesh=fine,
        in_specs=placed,
        out_specs=(
            P(ROWS, None),
            P(ROWS, None),
            P(("yx", "col"), "dp", None),
            P(("yx", "col"), "dp", None),
            P(("yx", "col"), "dp", None),
        ),
        check_vma=False,
    )
```

```python
import jax
import jax.numpy as jnp
from jax import lax
from jax.experimental import pallas as pl
from jax.experimental.pallas import tpu as pltpu
from jax.sharding import Mesh
from jax.sharding import PartitionSpec as P

SPLIT = 8
CHUNKS = 2
ROWS = ("dp", "yx", "col")
MESH_ID = pl.DeviceIdType.MESH
CONTRACT_LAST = (((1,), (1,)), ((), ()))
CONTRACT_FIRST = (((0,), (0,)), ((), ()))


def swap_kernel(src_ref, dst_ref, sems):
    other = 1 - lax.axis_index("dp")
    barrier = pltpu.get_barrier_semaphore()
    pl.semaphore_signal(barrier, 1, device_id={"dp": other}, device_id_type=MESH_ID)
    pl.semaphore_wait(barrier, 1)
    copy = pltpu.make_async_remote_copy(
        src_ref=src_ref,
        dst_ref=dst_ref,
        send_sem=sems.at[0],
        recv_sem=sems.at[1],
        device_id={"dp": other},
        device_id_type=MESH_ID,
    )
    copy.start()
    copy.wait()


def swap_with_partner(x, collective_id):
    size = x.size * x.dtype.itemsize
    return pl.pallas_call(
        swap_kernel,
        out_shape=jax.ShapeDtypeStruct(x.shape, x.dtype),
        in_specs=[pl.BlockSpec(memory_space=pl.ANY)],
        out_specs=pl.BlockSpec(memory_space=pl.ANY),
        scratch_shapes=[pltpu.SemaphoreType.DMA((2,))],
        compiler_params=pltpu.CompilerParams(collective_id=collective_id, has_side_effects=True),
        cost_estimate=pl.CostEstimate(flops=0, bytes_accessed=2 * size, transcendentals=0),
    )(x)


def own_batch(partial, collective_id):
    streams, rows, k = partial.shape
    split = partial.reshape(streams, SPLIT, 2, -1, k)
    traded = swap_with_partner(split[:, :, 1].astype(jnp.bfloat16), collective_id)
    return (split[:, :, 0] + traded.astype(jnp.float32)).reshape(streams, -1, k)


def all_batches(partial, collective_id):
    streams, rows, k = partial.shape
    split = partial.reshape(streams, SPLIT, 2, -1, k)
    traded = swap_with_partner(split.astype(jnp.bfloat16), collective_id)
    return (split + traded[:, :, ::-1].astype(jnp.float32)).reshape(streams, -1, k)


def both_batches(values, collective_id):
    traded = swap_with_partner(values, collective_id)
    streams, rows, k = values.shape
    mine = values.reshape(streams, SPLIT, 1, -1, k)
    theirs = traded.reshape(streams, SPLIT, 1, -1, k)
    return jnp.concatenate([mine, theirs], axis=2).reshape(streams, -1, k)


def trade_halves(arrived, shift, half, collective_id):
    rolled = jnp.roll(arrived, -shift, axis=-1)
    traded = swap_with_partner(rolled[..., half:], collective_id)
    return jnp.stack([rolled[..., :half], traded], axis=1)


def expert_chunk(arrived, shift, wg, wu, wd, first_id):
    half = wg.shape[0]
    shared = lax.all_gather(arrived, "col", axis=1, tiled=False)
    token_rows, cot_rows = shared.reshape(2, -1, half)
    partials = jnp.stack(
        [
            jnp.dot(token_rows, wg, preferred_element_type=jnp.float32),
            jnp.dot(token_rows, wu, preferred_element_type=jnp.float32),
            jnp.dot(cot_rows, wd, preferred_element_type=jnp.float32),
        ]
    )
    gate_pre, up_pre, hidden_grad = all_batches(partials, first_id + 1)
    gate_sigma = jax.nn.sigmoid(gate_pre)
    hidden_all = (gate_pre * gate_sigma * up_pre).astype(jnp.bfloat16)
    gate_all = (hidden_grad * up_pre * gate_sigma * (1.0 + gate_pre * (1.0 - gate_sigma))).astype(
        jnp.bfloat16
    )
    up_all = (hidden_grad * gate_pre * gate_sigma).astype(jnp.bfloat16)
    partial_value = lax.dot_general(
        hidden_all, wd, CONTRACT_LAST, preferred_element_type=jnp.float32
    ).astype(jnp.bfloat16)
    partial_grad = (
        lax.dot_general(gate_all, wg, CONTRACT_LAST, preferred_element_type=jnp.float32)
        + lax.dot_general(up_all, wu, CONTRACT_LAST, preferred_element_type=jnp.float32)
    ).astype(jnp.bfloat16)
    partial_rows = jnp.stack([partial_value, partial_grad])
    grad_terms = jnp.stack(
        [
            lax.dot_general(token_rows, gate_all, CONTRACT_FIRST, preferred_element_type=jnp.float32),
            lax.dot_general(token_rows, up_all, CONTRACT_FIRST, preferred_element_type=jnp.float32),
            lax.dot_general(cot_rows, hidden_all, CONTRACT_FIRST, preferred_element_type=jnp.float32),
        ]
    )
    return partial_rows, grad_terms


def bring_back(partial_rows, shift, collective_id, grads=None):
    half = partial_rows.shape[-1]
    summed = lax.psum_scatter(
        partial_rows.reshape(2, SPLIT, 2, -1, half), "col", scatter_dimension=1, tiled=True
    )[:, 0]
    if grads is not None:
        summed, grads = lax.optimization_barrier((summed, grads))
    traded_back = swap_with_partner(summed[:, 1], collective_id)
    rows = jnp.roll(jnp.concatenate([summed[:, 0], traded_back], axis=-1), shift, axis=-1)
    return rows, grads


def shards(tokens, routes, gate_values, gate_weight, up_weight, down_weight, cotangent):
    width = tokens.shape[1]
    half = gate_weight.shape[1]
    chosen = routes[0]
    scales = gate_values[0][:, :, None]
    shift = lax.axis_index("dp") * half
    wg, wu, wd = gate_weight[0], up_weight[0], down_weight[0]
    experts, slots = chosen.shape
    cut = slots // CHUNKS
    traded = []
    for k in range(CHUNKS):
        taken = chosen[:, k * cut : (k + 1) * cut]
        gains = scales[:, k * cut : (k + 1) * cut]
        scaled_cot = (gains * cotangent[taken].astype(jnp.float32)).astype(jnp.bfloat16)
        chunk = jnp.stack([tokens[taken], scaled_cot]).reshape(2, -1, width)
        if traded:
            chunk, _ = lax.optimization_barrier((chunk, traded[-1]))
        arrived = lax.all_to_all(chunk, "yx", split_axis=1, concat_axis=1, tiled=True)
        traded.append(trade_halves(arrived, shift, half, 4 * k))
    computed = [expert_chunk(traded[k], shift, wg, wu, wd, 4 * k) for k in range(CHUNKS)]
    grads = sum(c[1] for c in computed)
    backs = []
    for k in range(CHUNKS):
        last = k == CHUNKS - 1
        rows, finished = bring_back(computed[k][0], shift, 4 * k + 3, grads if last else None)
        if last:
            grads = finished
        back = lax.all_to_all(rows, "yx", split_axis=1, concat_axis=1, tiled=True)
        backs.append(back.reshape(2, experts, cut, width))
    back = jnp.concatenate(backs, axis=2).astype(jnp.float32)
    grads = grads.astype(jnp.bfloat16)
    layer_out = jnp.zeros((tokens.shape[0], width), jnp.float32).at[chosen].add(scales * back[0])
    token_grad = jnp.zeros((tokens.shape[0], width), jnp.float32).at[chosen].add(back[1])
    return (
        layer_out.astype(jnp.bfloat16),
        token_grad.astype(jnp.bfloat16),
        grads[0][None],
        grads[1][None],
        grads[2][None],
    )


def solution(mesh):
    n_dp, n_expert = mesh.devices.shape
    fine = Mesh(mesh.devices.reshape(n_dp, n_expert // SPLIT, SPLIT), ROWS)
    placed = (
        P(ROWS, None),
        P(ROWS, None, None),
        P(ROWS, None, None),
        P(("yx", "col"), "dp", None),
        P(("yx", "col"), "dp", None),
        P(("yx", "col"), "dp", None),
        P(ROWS, None),
    )
    return jax.shard_map(
        shards,
        mesh=fine,
        in_specs=placed,
        out_specs=(
            P(ROWS, None),
            P(ROWS, None),
            P(("yx", "col"), "dp", None),
            P(("yx", "col"), "dp", None),
            P(("yx", "col"), "dp", None),
        ),
        check_vma=False,
    )
```

```python
import jax
import jax.numpy as jnp
from jax import lax
from jax.experimental import pallas as pl
from jax.experimental.pallas import tpu as pltpu
from jax.sharding import Mesh
from jax.sharding import PartitionSpec as P

SPLIT = 8
CHUNKS = 2
ROWS = ("dp", "yx", "col")
MESH_ID = pl.DeviceIdType.MESH
CONTRACT_LAST = (((1,), (1,)), ((), ()))
CONTRACT_FIRST = (((0,), (0,)), ((), ()))


def swap_kernel(src_ref, dst_ref, sems):
    other = 1 - lax.axis_index("dp")
    barrier = pltpu.get_barrier_semaphore()
    pl.semaphore_signal(barrier, 1, device_id={"dp": other}, device_id_type=MESH_ID)
    pl.semaphore_wait(barrier, 1)
    lead = src_ref.shape[0]
    cut = lead // 2
    copies = []
    for i, (start, size) in enumerate(((0, cut), (cut, lead - cut))):
        copy = pltpu.make_async_remote_copy(
            src_ref=src_ref.at[pl.ds(start, size)],
            dst_ref=dst_ref.at[pl.ds(start, size)],
            send_sem=sems.at[2 * i],
            recv_sem=sems.at[2 * i + 1],
            device_id={"dp": other},
            device_id_type=MESH_ID,
        )
        copy.start()
        copies.append(copy)
    for copy in copies:
        copy.wait()


def swap_with_partner(x, collective_id):
    size = x.size * x.dtype.itemsize
    return pl.pallas_call(
        swap_kernel,
        out_shape=jax.ShapeDtypeStruct(x.shape, x.dtype),
        in_specs=[pl.BlockSpec(memory_space=pl.ANY)],
        out_specs=pl.BlockSpec(memory_space=pl.ANY),
        scratch_shapes=[pltpu.SemaphoreType.DMA((4,))],
        compiler_params=pltpu.CompilerParams(collective_id=collective_id, has_side_effects=True),
        cost_estimate=pl.CostEstimate(flops=0, bytes_accessed=2 * size, transcendentals=0),
    )(x)


def own_batch(partial, collective_id):
    streams, rows, k = partial.shape
    split = partial.reshape(streams, SPLIT, 2, -1, k)
    traded = swap_with_partner(split[:, :, 1].astype(jnp.bfloat16), collective_id)
    return (split[:, :, 0] + traded.astype(jnp.float32)).reshape(streams, -1, k)


def all_batches(partial, collective_id):
    streams, rows, k = partial.shape
    split = partial.reshape(streams, SPLIT, 2, -1, k)
    traded = swap_with_partner(split.astype(jnp.bfloat16), collective_id)
    return (split + traded[:, :, ::-1].astype(jnp.float32)).reshape(streams, -1, k)


def both_batches(values, collective_id):
    traded = swap_with_partner(values, collective_id)
    streams, rows, k = values.shape
    mine = values.reshape(streams, SPLIT, 1, -1, k)
    theirs = traded.reshape(streams, SPLIT, 1, -1, k)
    return jnp.concatenate([mine, theirs], axis=2).reshape(streams, -1, k)


def trade_halves(arrived, shift, half, collective_id):
    rolled = jnp.roll(arrived, -shift, axis=-1)
    traded = swap_with_partner(rolled[..., half:], collective_id)
    return jnp.stack([rolled[..., :half], traded], axis=1)


def expert_chunk(arrived, shift, wg, wu, wd, first_id):
    half = wg.shape[0]
    shared = lax.all_gather(arrived, "col", axis=1, tiled=False)
    token_rows, cot_rows = shared.reshape(2, -1, half)
    partials = jnp.stack(
        [
            jnp.dot(token_rows, wg, preferred_element_type=jnp.float32),
            jnp.dot(token_rows, wu, preferred_element_type=jnp.float32),
            jnp.dot(cot_rows, wd, preferred_element_type=jnp.float32),
        ]
    )
    gate_pre, up_pre, hidden_grad = all_batches(partials, first_id + 1)
    gate_sigma = jax.nn.sigmoid(gate_pre)
    hidden_all = (gate_pre * gate_sigma * up_pre).astype(jnp.bfloat16)
    gate_all = (hidden_grad * up_pre * gate_sigma * (1.0 + gate_pre * (1.0 - gate_sigma))).astype(
        jnp.bfloat16
    )
    up_all = (hidden_grad * gate_pre * gate_sigma).astype(jnp.bfloat16)
    partial_value = lax.dot_general(
        hidden_all, wd, CONTRACT_LAST, preferred_element_type=jnp.float32
    ).astype(jnp.bfloat16)
    partial_grad = (
        lax.dot_general(gate_all, wg, CONTRACT_LAST, preferred_element_type=jnp.float32)
        + lax.dot_general(up_all, wu, CONTRACT_LAST, preferred_element_type=jnp.float32)
    ).astype(jnp.bfloat16)
    partial_rows = jnp.stack([partial_value, partial_grad])
    grad_terms = jnp.stack(
        [
            lax.dot_general(token_rows, gate_all, CONTRACT_FIRST, preferred_element_type=jnp.float32),
            lax.dot_general(token_rows, up_all, CONTRACT_FIRST, preferred_element_type=jnp.float32),
            lax.dot_general(cot_rows, hidden_all, CONTRACT_FIRST, preferred_element_type=jnp.float32),
        ]
    )
    return partial_rows, grad_terms


def bring_back(partial_rows, shift, collective_id, grads=None):
    half = partial_rows.shape[-1]
    summed = lax.psum_scatter(
        partial_rows.reshape(2, SPLIT, 2, -1, half), "col", scatter_dimension=1, tiled=True
    )[:, 0]
    if grads is not None:
        summed, grads = lax.optimization_barrier((summed, grads))
    traded_back = swap_with_partner(summed[:, 1], collective_id)
    rows = jnp.roll(jnp.concatenate([summed[:, 0], traded_back], axis=-1), shift, axis=-1)
    return rows, grads


def shards(tokens, routes, gate_values, gate_weight, up_weight, down_weight, cotangent):
    width = tokens.shape[1]
    half = gate_weight.shape[1]
    chosen = routes[0]
    scales = gate_values[0][:, :, None]
    shift = lax.axis_index("dp") * half
    wg, wu, wd = gate_weight[0], up_weight[0], down_weight[0]
    experts, slots = chosen.shape
    cut = slots // CHUNKS
    traded = []
    for k in range(CHUNKS):
        taken = chosen[:, k * cut : (k + 1) * cut]
        gains = scales[:, k * cut : (k + 1) * cut]
        scaled_cot = (gains * cotangent[taken].astype(jnp.float32)).astype(jnp.bfloat16)
        chunk = jnp.stack([tokens[taken], scaled_cot]).reshape(2, -1, width)
        if traded:
            chunk, _ = lax.optimization_barrier((chunk, traded[-1]))
        arrived = lax.all_to_all(chunk, "yx", split_axis=1, concat_axis=1, tiled=True)
        traded.append(trade_halves(arrived, shift, half, 4 * k))
    computed = [expert_chunk(traded[k], shift, wg, wu, wd, 4 * k) for k in range(CHUNKS)]
    grads = sum(c[1] for c in computed)
    backs = []
    for k in range(CHUNKS):
        last = k == CHUNKS - 1
        rows, finished = bring_back(computed[k][0], shift, 4 * k + 3, grads if last else None)
        if last:
            grads = finished
        back = lax.all_to_all(rows, "yx", split_axis=1, concat_axis=1, tiled=True)
        backs.append(back.reshape(2, experts, cut, width))
    back = jnp.concatenate(backs, axis=2).astype(jnp.float32)
    grads = grads.astype(jnp.bfloat16)
    layer_out = jnp.zeros((tokens.shape[0], width), jnp.float32).at[chosen].add(scales * back[0])
    token_grad = jnp.zeros((tokens.shape[0], width), jnp.float32).at[chosen].add(back[1])
    return (
        layer_out.astype(jnp.bfloat16),
        token_grad.astype(jnp.bfloat16),
        grads[0][None],
        grads[1][None],
        grads[2][None],
    )


def solution(mesh):
    n_dp, n_expert = mesh.devices.shape
    fine = Mesh(mesh.devices.reshape(n_dp, n_expert // SPLIT, SPLIT), ROWS)
    placed = (
        P(ROWS, None),
        P(ROWS, None, None),
        P(ROWS, None, None),
        P(("yx", "col"), "dp", None),
        P(("yx", "col"), "dp", None),
        P(("yx", "col"), "dp", None),
        P(ROWS, None),
    )
    return jax.shard_map(
        shards,
        mesh=fine,
        in_specs=placed,
        out_specs=(
            P(ROWS, None),
            P(ROWS, None),
            P(("yx", "col"), "dp", None),
            P(("yx", "col"), "dp", None),
            P(("yx", "col"), "dp", None),
        ),
        check_vma=False,
    )
```
